512 devices in a mesh: tile: 64 (over z, y), lev: 8 (over x, core).
Axes of the slice: x: 4, y: 4, z: 16, core: 2. Of those that a mesh axis runs over, the one named last changes fastest.
Arguments:
- store: float32 [8, 4096, 8, 4, 128], P('lev', 'tile'), may hold values from -6 to 6
- placement: int32 [32, 4096], P('lev', 'tile'), may hold values from 0 to 511, as said below
- wet: int32 [4096, 128], P('tile'), may hold values 0 or 1
- kappa: float32 [32], P('lev'), may hold values from 0.1 to 1
- thickness: float32 [32], P('lev'), may hold values from 0.5 to 2
- cotangent: float32 [4, 32, 4096, 128], P(None, 'lev', 'tile'), may hold values from -6 to 6
Outputs:
- adjoint_state: float32 [4, 32, 4096, 128], P(None, 'lev', 'tile')
The draws below stay inside these ranges and needn't reach their ends.
Inputs may be any that keep to these rules, and one draw needn't show every extreme that they name: `placement`: within the 4 x 64 entries of one device the values are distinct; value v names slot v % 8 of holder tile v // 8 on the same level slab; in each device's block of 4 x 64 entries at least one holder tile supplies all 8 of its slots.
All inputs are finite; a program needn't handle non-finite values. No bound on the sum of `wet` on one device may be relied on, other than what follows from the above.
Results may differ from the reference program's by a relative error of at most 0.00002.
Values sent between devices are 32-bit elements; how exact they have to be, the bound alone decides.
A program may use at most 64 MiB of HBM per device.

```python
import math
import jax
import jax.numpy as jnp

LEV_DEV = 4
CX = 64
CY = 128
CAP = 8
NZ = 32
NX = 4096
N_TILE = 64
N_LEV = 8


def draw_placement(key, part):
    pieces = LEV_DEV * CX
    slots = N_TILE * CAP
    blocks = NZ // LEV_DEV * (NX // CX)

    def one_block(block_key):
        first, second, third = jax.random.split(block_key, 3)
        order = jax.random.permutation(first, slots).astype(jnp.int32)
        full_holder = jax.random.randint(second, (), 0, N_TILE).astype(jnp.int32)
        ids = jnp.arange(slots, dtype=jnp.int32)
        score = jnp.where(ids // CAP == full_holder, -1, order)
        chosen = jnp.argsort(score, stable=True)[:pieces].astype(jnp.int32)
        return jax.random.permutation(third, chosen).astype(jnp.int32)
    keys = jax.random.split(jax.random.fold_in(key, 7), blocks)
    table = jax.vmap(one_block)(keys)
    table = table.reshape(NZ // LEV_DEV, NX // CX, LEV_DEV, CX)
    return jnp.transpose(table, (0, 2, 1, 3)).reshape(NZ, NX).astype(jnp.int32)


def with_ends(array, stream_key, smallest, high):
    longest = array.shape.index(max(array.shape))
    spots = []
    for shift in (0, 1):
        where = [jax.random.randint(jax.random.fold_in(stream_key, axis), (), 0, length) for axis, length in enumerate(array.shape)]
        where[longest] = (where[longest] + shift) % array.shape[longest]
        spots.append(tuple(where))
    return array.at[spots[0]].set(smallest).at[spots[1]].set(high)


def block_levels(key, extent, cuts, least, top_value):
    def one(position, parts):
        heights = jax.random.uniform(jax.random.fold_in(jax.random.fold_in(key, 6), position), (parts,), jnp.float32, least / len(cuts), top_value / len(cuts))
        return jnp.repeat(jnp.exp(heights), extent[position] // parts).reshape((-1,) + (1,) * (len(extent) - position - 1))

    loudness = one(*cuts[0])
    for cut in cuts[1:]:
        loudness = loudness * one(*cut)
    return loudness


def gaussian(rng, shape, spread, reach, cuts=(), held_as=jnp.bfloat16):
    values = spread * jax.random.normal(rng, shape, jnp.float32)
    if cuts:
        values = values * block_levels(rng, shape, cuts, -0.22, 0.18)
    return jnp.clip(values, -reach, reach).astype(held_as)


def setup_inputs(seed: int = 0) -> dict:
    seeds = jax.random.split(jax.random.key(seed), 7)
    store = gaussian(seeds[0], (N_LEV, N_TILE * N_TILE, CAP, 4, CY), 1.0, 6.0, ((0, 8), (1, 64)), jnp.float32)
    placement = draw_placement(jax.random.fold_in(seeds[6], 71), 0)
    wet = with_ends((jax.random.randint(seeds[2], (NX, CY), 0, 4) < 3).astype(jnp.int32), jax.random.fold_in(seeds[2], 1), 0, 1)
    kappa = jnp.clip(jnp.exp(math.log(1.0) - 2.3025851 * jax.random.uniform(seeds[3], (NZ,), jnp.float32) ** block_levels(seeds[3], (NZ,), ((0, 8),), -0.2, 0.2)), 0.1, 1.0)
    thickness = jnp.clip(jnp.exp(math.log(2.0) - 1.3862944 * jax.random.uniform(seeds[4], (NZ,), jnp.float32) ** block_levels(seeds[4], (NZ,), ((0, 8),), -0.2, 0.2)), 0.5, 2.0)
    cotangent = gaussian(seeds[5], (4, NZ, NX, CY), 1.0, 6.0, ((1, 8), (2, 64)), jnp.float32)
    return dict(store=store, placement=placement, wet=wet, kappa=kappa, thickness=thickness, cotangent=cotangent)


def unpack(store, placement):
    level_slab = (jnp.arange(NZ, dtype=jnp.int32) // LEV_DEV)[:, None]
    owner = (jnp.arange(NX, dtype=jnp.int32) // CX)[None, :]
    holder = placement // CAP
    slot_index = placement % CAP
    rows = holder * N_TILE + owner
    picked = store[level_slab, rows, slot_index]
    return jnp.transpose(picked, (2, 0, 1, 3)).astype(jnp.float32)

def slope_x(field):
    return (jnp.roll(field, -1, 1) - jnp.roll(field, 1, 1)) * 0.5

def slope_y(field):
    return (jnp.roll(field, -1, 2) - jnp.roll(field, 1, 2)) * 0.5

def laplace(field):
    return jnp.roll(field, -1, 1) + jnp.roll(field, 1, 1) + jnp.roll(field, -1, 2) + jnp.roll(field, 1, 2) - 4.0 * field

def advance(state, wet, kappa, thickness):
    warmth, salinity, zonal, meridional = (state[0], state[1], state[2], state[3])
    density = -0.25 * warmth + 0.75 * salinity - 0.05 * warmth * warmth
    layered = density * thickness[:, None, None]
    pressure = 0.2 * (jnp.cumsum(layered, axis=0) - 0.5 * layered)
    ocean = wet.astype(jnp.float32)[None]
    diffuse = kappa[:, None, None]
    zonal_new = zonal + 0.2 * ocean * (-slope_x(pressure) + 0.5 * meridional)
    merid_new = meridional + 0.2 * ocean * (-slope_y(pressure) - 0.5 * zonal)
    warm_new = warmth + 0.2 * ocean * (diffuse * laplace(warmth) - zonal * slope_x(warmth) - meridional * slope_y(warmth))
    salt_new = salinity + 0.2 * ocean * (diffuse * laplace(salinity) - zonal * slope_x(salinity) - meridional * slope_y(salinity))
    return jnp.stack([warm_new, salt_new, zonal_new, merid_new])

def reference(store, placement, wet, kappa, thickness, cotangent):
    start_state = unpack(store, placement)

    def two_steps(state):
        return advance(advance(state, wet, kappa, thickness), wet, kappa, thickness)
    _, pullback = jax.vjp(two_steps, start_state)
    return pullback(cotangent)[0]
```

```python
import jax
import jax.numpy as jnp
from jax import lax
from jax.experimental import pallas as pl
from jax.experimental.pallas import tpu as pltpu
from jax.sharding import PartitionSpec as P

MESH = pl.DeviceIdType.MESH
LEVELS = 4
ROWS = 64
CELLS = 128
PAD = 72
EDGE = 4
SLOTS = 8
TILES = 64
RING = 16
SIDE = 4
SLABS = 8
HALO = 3
RIM = 2


def before(x):
    return pltpu.roll(x, 1, 0)


def after(x):
    return pltpu.roll(x, PAD - 1, 0)


def slope_x(x):
    return 0.5 * (after(x) - before(x))


def slope_y(x):
    return 0.5 * (pltpu.roll(x, CELLS - 1, 1) - pltpu.roll(x, 1, 1))


def stencil(x):
    down, up = after(x), before(x)
    right, left = pltpu.roll(x, CELLS - 1, 1), pltpu.roll(x, 1, 1)
    return 0.5 * (down - up), 0.5 * (right - left), (down + up) + (right + left) - 4.0 * x


def laplace(x):
    return stencil(x)[2]


def kernel(
    store, placement, wet, kappa, thickness, cotangent, out,
    slots, state, halo_out, halo_in, place, wet_in, scale, thick, cot, rim_out, rim_in,
    lam, mask, total, totals, both, boths,
    drive_p, mul_t, mul_s, base_t, base_s, base_u, base_v, bend,
    heat, layer, push_u, push_v, grad, later_t, later_s, adj_q, result,
    load_sem, ready_sem, slot_send, slot_recv, own_sem, halo_send, halo_recv,
    rim_send, rim_recv, total_send, total_recv, both_send, both_recv, out_sem,
):
    me = lax.axis_index("tile")
    lev = lax.axis_index("lev")
    z, y = me // SIDE, lax.rem(me, SIDE)

    def tile_at(dz, dy):
        return lax.rem(z + (dz + RING), RING) * SIDE + lax.rem(y + dy, SIDE)

    def signal(sem, **where):
        pl.semaphore_signal(sem, inc=1, device_id=where, device_id_type=MESH)

    greet = pltpu.get_barrier_semaphore()
    for dz in (1, -1, 2, -2):
        signal(greet, tile=tile_at(dz, 0))
    for dy in (1, 2, 3):
        signal(greet, tile=tile_at(0, dy))
    for k in range(1, SLABS):
        signal(greet, lev=lax.rem(lev + k, SLABS))

    loads = [
        pltpu.make_async_copy(cotangent, cot, load_sem.at[0]),
        pltpu.make_async_copy(wet, wet_in, load_sem.at[1]),
        pltpu.make_async_copy(placement, place, load_sem.at[2]),
        pltpu.make_async_copy(kappa, scale, load_sem.at[3]),
        pltpu.make_async_copy(thickness, thick, load_sem.at[4]),
    ]
    for load in loads:
        load.start()
    own = pltpu.make_async_copy(
        store.at[pl.ds(me * SLOTS, SLOTS)], slots.at[pl.ds(me * SLOTS, SLOTS)], own_sem
    )
    own.start()

    def send_slots(to):
        pltpu.make_async_remote_copy(
            src_ref=store.at[pl.ds(to * SLOTS, SLOTS)],
            dst_ref=slots.at[pl.ds(me * SLOTS, SLOTS)],
            send_sem=slot_send,
            recv_sem=slot_recv,
            device_id={"tile": to},
            device_id_type=MESH,
        ).start()

    def send_ring(first, last):
        @pl.loop(first * 8, last * 8)
        def _(i):
            reach = i // 8
            towards = 1 - 2 * lax.rem(i, 2)
            send_slots(tile_at(reach * towards, lax.rem(i // 2, SIDE)))

    for load in loads:
        load.wait()
    mask[EDGE : EDGE + ROWS] = 0.2 * wet_in[...].astype(jnp.float32)
    rim_out[0, 32:34] = 0.2 * wet_in[0:RIM].astype(jnp.float32)
    rim_out[1, 32:34] = 0.2 * wet_in[ROWS - RIM : ROWS].astype(jnp.float32)
    for f in range(4):
        for l in range(LEVELS):
            i = f * LEVELS + l
            lam[f, l, EDGE : EDGE + ROWS] = cot[f, l]
            rim_out[0, i * RIM : (i + 1) * RIM] = cot[f, l, 0:RIM]
            rim_out[1, i * RIM : (i + 1) * RIM] = cot[f, l, ROWS - RIM : ROWS]

    pl.semaphore_wait(greet, 7 + SLABS - 1)
    for dy in (1, 2, 3):
        signal(ready_sem.at[0], tile=tile_at(0, dy))
    for dy in (1, 2, 3):
        send_slots(tile_at(0, dy))
    pl.semaphore_wait(ready_sem.at[0], 3)
    for dz in (2, -2):
        signal(ready_sem.at[1], tile=tile_at(dz, 0))

    left, right = lax.rem(me + TILES - 1, TILES), lax.rem(me + 1, TILES)

    def to_neighbours(outgoing, incoming, send, recv):
        return [
            pltpu.make_async_remote_copy(
                src_ref=outgoing.at[side],
                dst_ref=incoming.at[side],
                send_sem=send.at[side],
                recv_sem=recv.at[side],
                device_id={"tile": to},
                device_id_type=MESH,
            )
            for side, to in ((0, left), (1, right))
        ]

    rims = to_neighbours(rim_out, rim_in, rim_send, rim_recv)
    for copy in rims:
        copy.start()
    send_ring(1, 3)
    pl.semaphore_wait(ready_sem.at[1], 2)
    for dz in (4, -4):
        signal(ready_sem.at[2], tile=tile_at(dz, 0))
    send_ring(3, 5)
    pl.semaphore_wait(ready_sem.at[2], 2)

    for copy in rims:
        copy.wait()
    for side, at in ((0, EDGE + ROWS), (1, EDGE - RIM)):
        mask[at : at + RIM] = rim_in[side, 32:34]
        for f in range(4):
            for l in range(LEVELS):
                i = f * LEVELS + l
                lam[f, l, at : at + RIM] = rim_in[side, i * RIM : (i + 1) * RIM]

    total[...] = jnp.zeros_like(total)

    @pl.loop(0, LEVELS)
    def _(l):
        m = mask[...]
        p = slope_x(m * lam[2, l]) + slope_y(m * lam[3, l])
        drive_p[l] = p
        total[...] += p

    def to_slabs(source, incoming, send, recv):
        for k in range(1, SLABS):
            to = lax.rem(lev + k, SLABS)
            pltpu.make_async_remote_copy(
                src_ref=source((lev + k) // SLABS),
                dst_ref=incoming.at[k - 1],
                send_sem=send,
                recv_sem=recv,
                device_id={"lev": to},
                device_id_type=MESH,
            ).start()

    def whole(ref, sem):
        pltpu.make_async_copy(ref, ref, sem).wait()

    to_slabs(lambda turn: total, totals, total_send, total_recv)

    for dy in range(SIDE):
        send_slots(tile_at(RING // 2, dy))

    @pl.loop(0, 24)
    def _(i):
        towards = 1 - 2 * lax.rem(i, 2)
        send_slots(tile_at((7 - i // 8) * towards, lax.rem(i // 2, SIDE)))

    whole(totals, total_recv)
    whole(totals, total_send)
    total_above = jnp.zeros((PAD, CELLS), jnp.float32)
    for k in range(1, SLABS):
        total_above += jnp.where(k > lev, totals[k - 1], 0.0)

    def second_step(j, running):
        l = LEVELS - 1 - j
        m = mask[...]
        p = drive_p[l]
        running = running + p
        density = 0.2 * (running - 0.5 * p) * thick[l]
        lt, ls, lu, lv = lam[0, l], lam[1, l], lam[2, l], lam[3, l]
        a, b = m * lt, m * ls
        mul_t[l] = a
        mul_s[l] = b
        base_t[l] = lt + scale[l] * laplace(a) - 0.25 * density
        base_s[l] = ls + scale[l] * laplace(b) + 0.75 * density
        base_u[l] = lu - 0.5 * (m * lv)
        base_v[l] = lv + 0.5 * (m * lu)
        bend[l] = 0.1 * density
        return running

    lax.fori_loop(0, LEVELS, second_step, total_above)

    own.wait()
    arrived = slots.at[pl.ds(0, (TILES - 1) * SLOTS)]
    whole(arrived, slot_recv)

    field = LEVELS * PAD
    for l in range(LEVELS):
        for r in range(HALO):
            halo_out[0, l * HALO + r] = slots[place[l, r]]
            halo_out[1, l * HALO + r] = slots[place[l, ROWS - HALO + r]]
    halos = to_neighbours(halo_out, halo_in, halo_send, halo_recv)
    for copy in halos:
        copy.start()

    for l in range(LEVELS):

        @pl.loop(0, ROWS // 8)
        def _(g):
            for r in range(8):
                at = l * PAD + EDGE + g * 8 + r
                state[pl.ds(at, 4, stride=field), :] = slots[place[l, g * 8 + r]]

    for copy in halos:
        copy.wait()
    for side, at in ((0, EDGE + ROWS), (1, EDGE - HALO)):
        for l in range(LEVELS):
            for r in range(HALO):
                state[pl.ds(l * PAD + at + r, 4, stride=field), :] = halo_in[side, l * HALO + r]

    def start_field(f, l):
        return state[pl.ds(pl.multiple_of(f * field + l * PAD, 8), PAD), :]

    both[...] = jnp.zeros_like(both)

    @pl.loop(0, LEVELS)
    def _(l):
        m = mask[...]
        t, s, u, v = (start_field(f, l) for f in range(4))
        tx, ty, tl = stencil(t)
        sx, sy, sl = stencil(s)
        t1 = t + m * (scale[l] * tl - u * tx - v * ty)
        s1 = s + m * (scale[l] * sl - u * sx - v * sy)
        q = (-0.25 * t + 0.75 * s - 0.05 * t * t) * thick[l]
        layer[l] = q
        both[0] += q
        heat[l] = t1
        grad[0, l] = tx
        grad[1, l] = ty
        grad[2, l] = sx
        grad[3, l] = sy
        a, b = mul_t[l], mul_s[l]
        mu = base_u[l] - a * slope_x(t1) - b * slope_x(s1)
        mv = base_v[l] - a * slope_y(t1) - b * slope_y(s1)
        c, d = m * mu, m * mv
        push_u[l] = mu - 0.5 * d
        push_v[l] = mv + 0.5 * c
        p = slope_x(c) + slope_y(d)
        drive_p[l] = p
        both[1] += p

    to_slabs(lambda turn: both.at[turn], boths, both_send, both_recv)

    def inner(l, running):
        m = mask[...]
        q = layer[l]
        running = running + q
        pressure = 0.2 * (running - 0.5 * q)
        u, v = start_field(2, l), start_field(3, l)
        u1 = u + m * (0.5 * v - slope_x(pressure))
        v1 = v - m * (0.5 * u + slope_y(pressure))
        a, b = mul_t[l], mul_s[l]
        later_t[l] = base_t[l] - bend[l] * heat[l] + slope_x(a * u1) + slope_y(a * v1)
        later_s[l] = base_s[l] + slope_x(b * u1) + slope_y(b * v1)
        return running

    lax.fori_loop(0, LEVELS, inner, jnp.zeros((PAD, CELLS), jnp.float32))

    def upward(j, running):
        l = LEVELS - 1 - j
        p = drive_p[l]
        running = running + p
        adj_q[l] = running - 0.5 * p
        return running

    lax.fori_loop(0, LEVELS, upward, jnp.zeros((PAD, CELLS), jnp.float32))

    whole(boths, both_recv)
    upper = jnp.zeros((PAD, CELLS), jnp.float32)
    lower = jnp.zeros((PAD, CELLS), jnp.float32)
    for k in range(1, SLABS):
        came = boths[k - 1]
        upper += jnp.where(k <= lev, came, 0.0)
        lower += jnp.where(k > lev, came, 0.0)
    m = mask[...]
    total[...] = lower
    totals[0] = 0.2 * m * slope_x(upper)
    totals[1] = 0.2 * m * slope_y(upper)

    @pl.loop(0, LEVELS)
    def _(l):
        m = mask[...]
        gx, gy = totals[0], totals[1]
        a, b = mul_t[l], mul_s[l]
        mt = later_t[l] - slope_x(a * gx) - slope_y(a * gy)
        ms = later_s[l] - slope_x(b * gx) - slope_y(b * gy)
        a, b = m * mt, m * ms
        t, u, v = start_field(0, l), start_field(2, l), start_field(3, l)
        density = 0.2 * (adj_q[l] + total[...]) * thick[l]
        here = slice(EDGE, EDGE + ROWS)
        out_t = mt + scale[l] * laplace(a) + slope_x(a * u) + slope_y(a * v) - density * (0.25 + 0.1 * t)
        out_s = ms + scale[l] * laplace(b) + slope_x(b * u) + slope_y(b * v) + 0.75 * density
        out_u = push_u[l] - a * grad[0, l] - b * grad[2, l]
        out_v = push_v[l] - a * grad[1, l] - b * grad[3, l]
        result[0, l] = out_t[here]
        result[1, l] = out_s[here]
        result[2, l] = out_u[here]
        result[3, l] = out_v[here]

    finish = pltpu.make_async_copy(result, out, out_sem)
    finish.start()
    whole(arrived, slot_send)
    whole(boths, both_send)
    finish.wait()


def per_device(store, placement, wet, kappa, thickness, cotangent):
    padded = pltpu.VMEM((LEVELS, PAD, CELLS), jnp.float32)
    plane = pltpu.VMEM((PAD, CELLS), jnp.float32)
    planes = pltpu.VMEM((SLABS - 1, PAD, CELLS), jnp.float32)
    dma = pltpu.SemaphoreType.DMA
    scratch = [
        pltpu.VMEM((TILES * SLOTS, 4, CELLS), jnp.float32),
        pltpu.VMEM((4 * LEVELS * PAD, CELLS), jnp.float32),
        pltpu.VMEM((2, LEVELS * HALO, 4, CELLS), jnp.float32),
        pltpu.VMEM((2, LEVELS * HALO, 4, CELLS), jnp.float32),
        pltpu.SMEM((LEVELS, ROWS), jnp.int32),
        pltpu.VMEM((ROWS, CELLS), jnp.int32),
        pltpu.SMEM((LEVELS,), jnp.float32),
        pltpu.SMEM((LEVELS,), jnp.float32),
        pltpu.VMEM((4, LEVELS, ROWS, CELLS), jnp.float32),
        pltpu.VMEM((2, 40, CELLS), jnp.float32),
        pltpu.VMEM((2, 40, CELLS), jnp.float32),
        pltpu.VMEM((4, LEVELS, PAD, CELLS), jnp.float32),
        plane,
        plane,
        planes,
        pltpu.VMEM((2, PAD, CELLS), jnp.float32),
        planes,
        padded, padded, padded, padded, padded, padded, padded, padded,
        padded, padded, padded, padded,
        pltpu.VMEM((4, LEVELS, PAD, CELLS), jnp.float32),
        padded, padded, padded,
        pltpu.VMEM((4, LEVELS, ROWS, CELLS), jnp.float32),
        dma((5,)),
        pltpu.SemaphoreType.REGULAR((3,)),
        dma, dma, dma,
        dma((2,)), dma((2,)), dma((2,)), dma((2,)),
        dma, dma, dma, dma, dma,
    ]
    return pl.pallas_call(
        kernel,
        out_shape=jax.ShapeDtypeStruct(cotangent.shape, jnp.float32),
        in_specs=[pl.BlockSpec(memory_space=pl.ANY)] * 6,
        out_specs=pl.BlockSpec(memory_space=pl.ANY),
        scratch_shapes=scratch,
        compiler_params=pltpu.CompilerParams(
            collective_id=0, has_side_effects=True, vmem_limit_bytes=32 << 20
        ),
    )(
        store.reshape(TILES * SLOTS, 4, CELLS), placement, wet, kappa, thickness, cotangent
    )


def solution(mesh):
    placed = (
        P("lev", "tile", None, None, None),
        P("lev", "tile"),
        P("tile", None),
        P("lev"),
        P("lev"),
        P(None, "lev", "tile", None),
    )
    return jax.shard_map(
        per_device,
        mesh=mesh,
        in_specs=placed,
        out_specs=P(None, "lev", "tile", None),
        check_vma=False,
    )
```

```python
import functools

import jax
import jax.numpy as jnp
from jax import lax
from jax.experimental import pallas as pl
from jax.experimental.pallas import tpu as pltpu
from jax.sharding import PartitionSpec as P

MESH = pl.DeviceIdType.MESH
LEVELS = 4
ROWS = 64
CELLS = 128
PAD = 72
EDGE = 4
SLOTS = 8
TILES = 64
RING = 16
SIDE = 4
SLABS = 8
HALO = 3
EARLY = (0, 1, 2, 3, 4)
ORDER = (0, 1, 2, 3, 4, 5, 6, 15, 7, 14, 13, 8, 12, 9, 10, 11)
SPLIT = 5
NEAR = 4
RIM = 2


def before(x):
    return pltpu.roll(x, 1, 0)


def after(x):
    return pltpu.roll(x, x.shape[0] - 1, 0)


def slope_x(x):
    return 0.5 * (after(x) - before(x))


def slope_y(x):
    return 0.5 * (pltpu.roll(x, CELLS - 1, 1) - pltpu.roll(x, 1, 1))


def stencil(x):
    down, up = after(x), before(x)
    right, left = pltpu.roll(x, CELLS - 1, 1), pltpu.roll(x, 1, 1)
    return 0.5 * (down - up), 0.5 * (right - left), (down + up) + (right + left) - 4.0 * x


def laplace(x):
    return stencil(x)[2]


def kernel(
    store, placement, wet, kappa, thickness, cotangent, out,
    slots, state, halo_out, halo_in, place, wet_in, scale, thick, cot, rim_out, rim_in,
    lam, mask, total, totals, both, mid, mids, edge, edges,
    drive_p, mul_t, mul_s, base_t, base_s, base_u, base_v, bend,
    heat, layer, push_u, push_v, grad, later_t, later_s, adj_q, result,
    load_sem, ready_sem, slot_send, slot_recv, own_sem, halo_send, halo_recv,
    rim_send, rim_recv, total_send, total_recv, mid_send, mid_recv, edge_send, edge_recv, out_sem,
):
    me = lax.axis_index("tile")
    lev = lax.axis_index("lev")
    z, y = me // SIDE, lax.rem(me, SIDE)

    def tile_at(dz, dy):
        return lax.rem(z + (dz + RING), RING) * SIDE + lax.rem(y + dy, SIDE)

    def signal(sem, **where):
        pl.semaphore_signal(sem, inc=1, device_id=where, device_id_type=MESH)

    greet = pltpu.get_barrier_semaphore()
    for dz in (1, -1, 2, -2):
        signal(greet, tile=tile_at(dz, 0))
    for dy in (1, 2, 3):
        signal(greet, tile=tile_at(0, dy))
    for k in range(1, SLABS):
        signal(greet, lev=lax.rem(lev + k, SLABS))

    loads = [
        pltpu.make_async_copy(cotangent, cot, load_sem.at[0]),
        pltpu.make_async_copy(wet, wet_in, load_sem.at[1]),
        pltpu.make_async_copy(placement, place, load_sem.at[2]),
        pltpu.make_async_copy(kappa, scale, load_sem.at[3]),
        pltpu.make_async_copy(thickness, thick, load_sem.at[4]),
    ]
    for load in loads:
        load.start()

    def is_early(plane):
        return functools.reduce(lambda found, e: found | (plane == e), EARLY, plane < 0)

    own = pltpu.make_async_copy(
        store.at[pl.ds(me * SLOTS, SLOTS)], slots.at[pl.ds(me * SLOTS, SLOTS)], own_sem
    )
    own.start()

    def send_slots(to):
        pltpu.make_async_remote_copy(
            src_ref=store.at[pl.ds(to * SLOTS, SLOTS)],
            dst_ref=slots.at[pl.ds(me * SLOTS, SLOTS)],
            send_sem=slot_send,
            recv_sem=slot_recv,
            device_id={"tile": to},
            device_id_type=MESH,
        ).start()

    def send_near(reach):
        for dz in (reach, -reach):
            to_z = lax.rem(z + (dz + RING), RING)

            @pl.when(is_early(to_z) if reach > 2 else z >= 0)
            def _():
                @pl.loop(0, SIDE)
                def _(dy):
                    send_slots(tile_at(dz, dy))

    def send_planes(planes):
        for to_z in planes:
            gap = lax.rem(z + (RING - to_z), RING)
            gap = jnp.minimum(gap, RING - gap)

            @pl.when(gap > (NEAR if to_z in EARLY else 2))
            def _():
                @pl.loop(0, SIDE)
                def _(dy):
                    if to_z == RING - 1:

                        @pl.when(dy > 0)
                        def _():
                            send_slots(to_z * SIDE + dy - 1)
                    else:
                        send_slots(to_z * SIDE + lax.rem(y + dy, SIDE))

    pl.semaphore_wait(greet, 7 + SLABS - 1)
    for dy in (1, 2, 3):
        signal(ready_sem.at[0], tile=tile_at(0, dy))
    for dy in (1, 2, 3):
        send_slots(tile_at(0, dy))
    pl.semaphore_wait(ready_sem.at[0], 3)
    for dz in (2, -2):
        signal(ready_sem.at[1], tile=tile_at(dz, 0))
    send_near(1)
    send_near(2)

    for load in loads:
        load.wait()
    mask[EDGE : EDGE + ROWS] = 0.2 * wet_in[...].astype(jnp.float32)
    rim_out[0, 32:34] = 0.2 * wet_in[0:RIM].astype(jnp.float32)
    rim_out[1, 32:34] = 0.2 * wet_in[ROWS - RIM : ROWS].astype(jnp.float32)
    for f in range(4):
        for l in range(LEVELS):
            i = f * LEVELS + l
            lam[f, l, EDGE : EDGE + ROWS] = cot[f, l]
            rim_out[0, i * RIM : (i + 1) * RIM] = cot[f, l, 0:RIM]
            rim_out[1, i * RIM : (i + 1) * RIM] = cot[f, l, ROWS - RIM : ROWS]

    left, right = lax.rem(me + TILES - 1, TILES), lax.rem(me + 1, TILES)

    def to_neighbours(outgoing, incoming, send, recv):
        return [
            pltpu.make_async_remote_copy(
                src_ref=outgoing.at[side],
                dst_ref=incoming.at[side],
                send_sem=send.at[side],
                recv_sem=recv.at[side],
                device_id={"tile": to},
                device_id_type=MESH,
            )
            for side, to in ((0, left), (1, right))
        ]

    rims = to_neighbours(rim_out, rim_in, rim_send, rim_recv)
    for copy in rims:
        copy.start()

    pl.semaphore_wait(ready_sem.at[1], 2)
    for dz in (4, -4):
        signal(ready_sem.at[2], tile=tile_at(dz, 0))
    send_near(3)
    send_near(4)
    pl.semaphore_wait(ready_sem.at[2], 2)
    @pl.when((z < RING - 1 - 2) & (z > 1))
    def _():
        send_slots(TILES - 1)

    send_planes(ORDER[:SPLIT])

    for copy in rims:
        copy.wait()
    for side, at in ((0, EDGE + ROWS), (1, EDGE - RIM)):
        mask[at : at + RIM] = rim_in[side, 32:34]
        for f in range(4):
            for l in range(LEVELS):
                i = f * LEVELS + l
                lam[f, l, at : at + RIM] = rim_in[side, i * RIM : (i + 1) * RIM]

    total[...] = jnp.zeros_like(total)

    @pl.loop(0, LEVELS)
    def _(l):
        m = mask[...]
        p = slope_x(m * lam[2, l]) + slope_y(m * lam[3, l])
        drive_p[l] = p
        total[...] += p

    def to_slabs(source, incoming, send, recv):
        for k in range(1, SLABS):
            to = lax.rem(lev + k, SLABS)
            pltpu.make_async_remote_copy(
                src_ref=source((lev + k) // SLABS),
                dst_ref=incoming.at[k - 1],
                send_sem=send,
                recv_sem=recv,
                device_id={"lev": to},
                device_id_type=MESH,
            ).start()

    def whole(ref, sem):
        pltpu.make_async_copy(ref, ref, sem).wait()

    to_slabs(lambda turn: total, totals, total_send, total_recv)

    send_planes(ORDER[SPLIT:])

    whole(totals, total_recv)
    whole(totals, total_send)
    total_above = jnp.zeros((PAD, CELLS), jnp.float32)
    for k in range(1, SLABS):
        total_above += jnp.where(k > lev, totals[k - 1], 0.0)

    def second_step(j, running):
        l = LEVELS - 1 - j
        m = mask[...]
        p = drive_p[l]
        running = running + p
        density = 0.2 * (running - 0.5 * p) * thick[l]
        lt, ls, lu, lv = lam[0, l], lam[1, l], lam[2, l], lam[3, l]
        a, b = m * lt, m * ls
        mul_t[l] = a
        mul_s[l] = b
        base_t[l] = lt + scale[l] * laplace(a) - 0.25 * density
        base_s[l] = ls + scale[l] * laplace(b) + 0.75 * density
        base_u[l] = lu - 0.5 * (m * lv)
        base_v[l] = lv + 0.5 * (m * lu)
        bend[l] = 0.1 * density
        return running

    lax.fori_loop(0, LEVELS, second_step, total_above)

    own.wait()
    arrived = slots.at[pl.ds(0, (TILES - 1) * SLOTS)]
    whole(arrived, slot_recv)

    field = LEVELS * PAD
    for l in range(LEVELS):
        for r in range(HALO):
            halo_out[0, l * HALO + r] = slots[place[l, r]]
            halo_out[1, l * HALO + r] = slots[place[l, ROWS - HALO + r]]
    halos = to_neighbours(halo_out, halo_in, halo_send, halo_recv)
    for copy in halos:
        copy.start()

    for l in range(LEVELS):

        @pl.loop(0, ROWS // 8)
        def _(g):
            for r in range(8):
                at = l * PAD + EDGE + g * 8 + r
                state[pl.ds(at, 4, stride=field), :] = slots[place[l, g * 8 + r]]

    def start_field(f, l):
        return state[pl.ds(pl.multiple_of(f * field + l * PAD, 8), PAD), :]

    def first_step(l, cut):
        m = cut(mask[...])
        t, s, u, v = (cut(start_field(f, l)) for f in range(4))
        tx, ty, tl = stencil(t)
        sx, sy, sl = stencil(s)
        t1 = t + m * (scale[l] * tl - u * tx - v * ty)
        s1 = s + m * (scale[l] * sl - u * sx - v * sy)
        q = (-0.25 * t + 0.75 * s - 0.05 * t * t) * thick[l]
        a, b = cut(mul_t[l]), cut(mul_s[l])
        mu = cut(base_u[l]) - a * slope_x(t1) - b * slope_x(s1)
        mv = cut(base_v[l]) - a * slope_y(t1) - b * slope_y(s1)
        c, d = m * mu, m * mv
        p = slope_x(c) + slope_y(d)
        return q, t1, tx, ty, sx, sy, mu - 0.5 * d, mv + 0.5 * c, p

    kept = (
        layer, heat, grad.at[0], grad.at[1], grad.at[2], grad.at[3], push_u, push_v, drive_p,
    )

    mid[...] = jnp.zeros_like(mid)

    @pl.loop(0, LEVELS)
    def _(l):
        values = first_step(l, lambda x: x)
        for ref, value in zip(kept, values):
            ref[l] = value
        mid[0] += values[0][8 : PAD - 8]
        mid[1] += values[-1][8 : PAD - 8]

    to_slabs(lambda turn: mid.at[turn], mids, mid_send, mid_recv)

    for copy in halos:
        copy.wait()
    for side, at in ((0, EDGE + ROWS), (1, EDGE - HALO)):
        for l in range(LEVELS):
            for r in range(HALO):
                state[pl.ds(l * PAD + at + r, 4, stride=field), :] = halo_in[side, l * HALO + r]

    edge[...] = jnp.zeros_like(edge)

    @pl.loop(0, LEVELS)
    def _(l):
        values = first_step(l, lambda x: jnp.concatenate([x[:16], x[PAD - 16 :]], 0))
        for ref, value in zip(kept, values):
            ref[l, :8] = value[:8]
            ref[l, PAD - 8 :] = value[24:]
        for side, value in ((0, values[0]), (1, values[-1])):
            edge[side, :8] += value[:8]
            edge[side, 8:] += value[24:]

    to_slabs(lambda turn: edge.at[turn], edges, edge_send, edge_recv)

    def inner(l, running):
        m = mask[...]
        q = layer[l]
        running = running + q
        pressure = 0.2 * (running - 0.5 * q)
        u, v = start_field(2, l), start_field(3, l)
        u1 = u + m * (0.5 * v - slope_x(pressure))
        v1 = v - m * (0.5 * u + slope_y(pressure))
        a, b = mul_t[l], mul_s[l]
        later_t[l] = base_t[l] - bend[l] * heat[l] + slope_x(a * u1) + slope_y(a * v1)
        later_s[l] = base_s[l] + slope_x(b * u1) + slope_y(b * v1)
        return running

    lax.fori_loop(0, LEVELS, inner, jnp.zeros((PAD, CELLS), jnp.float32))

    def upward(j, running):
        l = LEVELS - 1 - j
        p = drive_p[l]
        running = running + p
        adj_q[l] = running - 0.5 * p
        return running

    lax.fori_loop(0, LEVELS, upward, jnp.zeros((PAD, CELLS), jnp.float32))

    def gather_totals(came):
        upper = jnp.zeros(came.shape[1:], jnp.float32)
        lower = jnp.zeros(came.shape[1:], jnp.float32)
        for k in range(1, SLABS):
            upper += jnp.where(k <= lev, came[k - 1], 0.0)
            lower += jnp.where(k > lev, came[k - 1], 0.0)
        return upper, lower

    whole(mids, mid_recv)
    for i, value in enumerate(gather_totals(mids)):
        both[i, 8 : PAD - 8] = value
    whole(edges, edge_recv)
    for i, value in enumerate(gather_totals(edges)):
        both[i, :8] = value[:8]
        both[i, PAD - 8 :] = value[8:]
    m, upper = mask[...], both[0]
    totals[0] = 0.2 * m * slope_x(upper)
    totals[1] = 0.2 * m * slope_y(upper)

    @pl.loop(0, LEVELS)
    def _(l):
        m = mask[...]
        gx, gy = totals[0], totals[1]
        a, b = mul_t[l], mul_s[l]
        mt = later_t[l] - slope_x(a * gx) - slope_y(a * gy)
        ms = later_s[l] - slope_x(b * gx) - slope_y(b * gy)
        a, b = m * mt, m * ms
        t, u, v = start_field(0, l), start_field(2, l), start_field(3, l)
        density = 0.2 * (adj_q[l] + both[1]) * thick[l]
        here = slice(EDGE, EDGE + ROWS)
        out_t = mt + scale[l] * laplace(a) + slope_x(a * u) + slope_y(a * v) - density * (0.25 + 0.1 * t)
        out_s = ms + scale[l] * laplace(b) + slope_x(b * u) + slope_y(b * v) + 0.75 * density
        out_u = push_u[l] - a * grad[0, l] - b * grad[2, l]
        out_v = push_v[l] - a * grad[1, l] - b * grad[3, l]
        result[0, l] = out_t[here]
        result[1, l] = out_s[here]
        result[2, l] = out_u[here]
        result[3, l] = out_v[here]
        pltpu.make_async_copy(result.at[:, l], out.at[:, l], out_sem.at[l]).start()

    whole(arrived, slot_send)
    whole(mids, mid_send)
    whole(edges, edge_send)
    for l in range(LEVELS):
        pltpu.make_async_copy(result.at[:, l], out.at[:, l], out_sem.at[l]).wait()


def per_device(store, placement, wet, kappa, thickness, cotangent):
    padded = pltpu.VMEM((LEVELS, PAD, CELLS), jnp.float32)
    plane = pltpu.VMEM((PAD, CELLS), jnp.float32)
    planes = pltpu.VMEM((SLABS - 1, PAD, CELLS), jnp.float32)
    dma = pltpu.SemaphoreType.DMA
    scratch = [
        pltpu.VMEM((TILES * SLOTS, 4, CELLS), jnp.float32),
        pltpu.VMEM((4 * LEVELS * PAD, CELLS), jnp.float32),
        pltpu.VMEM((2, LEVELS * HALO, 4, CELLS), jnp.float32),
        pltpu.VMEM((2, LEVELS * HALO, 4, CELLS), jnp.float32),
        pltpu.SMEM((LEVELS, ROWS), jnp.int32),
        pltpu.VMEM((ROWS, CELLS), jnp.int32),
        pltpu.SMEM((LEVELS,), jnp.float32),
        pltpu.SMEM((LEVELS,), jnp.float32),
        pltpu.VMEM((4, LEVELS, ROWS, CELLS), jnp.float32),
        pltpu.VMEM((2, 40, CELLS), jnp.float32),
        pltpu.VMEM((2, 40, CELLS), jnp.float32),
        pltpu.VMEM((4, LEVELS, PAD, CELLS), jnp.float32),
        plane,
        plane,
        planes,
        pltpu.VMEM((2, PAD, CELLS), jnp.float32),
        pltpu.VMEM((2, PAD - 16, CELLS), jnp.float32),
        pltpu.VMEM((SLABS - 1, PAD - 16, CELLS), jnp.float32),
        pltpu.VMEM((2, 16, CELLS), jnp.float32),
        pltpu.VMEM((SLABS - 1, 16, CELLS), jnp.float32),
        padded, padded, padded, padded, padded, padded, padded, padded,
        padded, padded, padded, padded,
        pltpu.VMEM((4, LEVELS, PAD, CELLS), jnp.float32),
        padded, padded, padded,
        pltpu.VMEM((4, LEVELS, ROWS, CELLS), jnp.float32),
        dma((5,)),
        pltpu.SemaphoreType.REGULAR((3,)),
        dma, dma, dma,
        dma((2,)), dma((2,)), dma((2,)), dma((2,)),
        dma, dma, dma, dma, dma, dma,
        dma((LEVELS,)),
    ]
    return pl.pallas_call(
        kernel,
        out_shape=jax.ShapeDtypeStruct(cotangent.shape, jnp.float32),
        in_specs=[pl.BlockSpec(memory_space=pltpu.HBM)] * 6,
        out_specs=pl.BlockSpec(memory_space=pltpu.HBM),
        scratch_shapes=scratch,
        compiler_params=pltpu.CompilerParams(
            collective_id=0, has_side_effects=True, vmem_limit_bytes=60 << 20
        ),
    )(
        store.reshape(TILES * SLOTS, 4, CELLS), placement, wet, kappa, thickness, cotangent
    )


def solution(mesh):
    placed = (
        P("lev", "tile", None, None, None),
        P("lev", "tile"),
        P("tile", None),
        P("lev"),
        P("lev"),
        P(None, "lev", "tile", None),
    )
    return jax.shard_map(
        per_device,
        mesh=mesh,
        in_specs=placed,
        out_specs=P(None, "lev", "tile", None),
        check_vma=False,
    )
```

```python
import functools

import jax
import jax.numpy as jnp
from jax import lax
from jax.experimental import pallas as pl
from jax.experimental.pallas import tpu as pltpu
from jax.sharding import PartitionSpec as P

MESH = pl.DeviceIdType.MESH
LEVELS = 4
ROWS = 64
CELLS = 128
PAD = 72
EDGE = 4
SLOTS = 8
TILES = 64
RING = 16
SIDE = 4
SLABS = 8
HALO = 3
EARLY = (0, 1, 2, 3)
ORDER = (0, 1, 2, 3, 4, 5, 6, 15, 7, 14, 13, 8, 12, 9, 10, 11)
SPLIT = 5
NEAR = 4
UNROLL = True
RIM = 2


def before(x):
    return pltpu.roll(x, 1, 0)


def after(x):
    return pltpu.roll(x, x.shape[0] - 1, 0)


def slope_x(x):
    return 0.5 * (after(x) - before(x))


def slope_y(x):
    return 0.5 * (pltpu.roll(x, CELLS - 1, 1) - pltpu.roll(x, 1, 1))


def stencil(x):
    down, up = after(x), before(x)
    right, left = pltpu.roll(x, CELLS - 1, 1), pltpu.roll(x, 1, 1)
    return 0.5 * (down - up), 0.5 * (right - left), (down + up) + (right + left) - 4.0 * x


def laplace(x):
    return stencil(x)[2]


def kernel(
    store, placement, wet, kappa, thickness, cotangent, out,
    slots, state, halo_out, halo_in, place, wet_in, scale, thick, cot, rim_out, rim_in,
    lam, mask, total, totals, both, mid, mids, edge, edges,
    drive_p, mul_t, mul_s, base_t, base_s, base_u, base_v, bend,
    heat, layer, push_u, push_v, grad, later_t, later_s, adj_q, moved,
    load_sem, ready_sem, slot_send, slot_recv, own_sem, halo_send, halo_recv,
    rim_send, rim_recv, total_send, total_recv, mid_send, mid_recv, edge_send, edge_recv,
):
    me = lax.axis_index("tile")
    lev = lax.axis_index("lev")
    z, y = me // SIDE, lax.rem(me, SIDE)

    def tile_at(dz, dy):
        return lax.rem(z + (dz + RING), RING) * SIDE + lax.rem(y + dy, SIDE)

    def signal(sem, **where):
        pl.semaphore_signal(sem, inc=1, device_id=where, device_id_type=MESH)

    greet = pltpu.get_barrier_semaphore()
    for dz in (1, -1, 2, -2):
        signal(greet, tile=tile_at(dz, 0))
    for dy in (1, 2, 3):
        signal(greet, tile=tile_at(0, dy))
    for k in range(1, SLABS):
        signal(greet, lev=lax.rem(lev + k, SLABS))

    loads = [
        pltpu.make_async_copy(cotangent, cot, load_sem.at[0]),
        pltpu.make_async_copy(wet, wet_in, load_sem.at[1]),
        pltpu.make_async_copy(placement, place, load_sem.at[2]),
        pltpu.make_async_copy(kappa, scale, load_sem.at[3]),
        pltpu.make_async_copy(thickness, thick, load_sem.at[4]),
    ]
    for load in loads:
        load.start()

    def is_early(plane):
        return functools.reduce(lambda found, e: found | (plane == e), EARLY, plane < 0)

    own = pltpu.make_async_copy(
        store.at[pl.ds(me * SLOTS, SLOTS)], slots.at[pl.ds(me * SLOTS, SLOTS)], own_sem
    )
    own.start()

    def send_slots(to):
        pltpu.make_async_remote_copy(
            src_ref=store.at[pl.ds(to * SLOTS, SLOTS)],
            dst_ref=slots.at[pl.ds(me * SLOTS, SLOTS)],
            send_sem=slot_send,
            recv_sem=slot_recv,
            device_id={"tile": to},
            device_id_type=MESH,
        ).start()

    def send_near(reach):
        for dz in (reach, -reach):
            to_z = lax.rem(z + (dz + RING), RING)

            @pl.when(is_early(to_z) if reach > 2 else z >= 0)
            def _():
                @pl.loop(0, SIDE)
                def _(dy):
                    send_slots(tile_at(dz, dy))

    def send_planes(planes):
        for to_z in planes:
            gap = lax.rem(z + (RING - to_z), RING)
            gap = jnp.minimum(gap, RING - gap)

            @pl.when(gap > (NEAR if to_z in EARLY else 2))
            def _():
                @pl.loop(0, SIDE)
                def _(dy):
                    if to_z == RING - 1:

                        @pl.when(dy > 0)
                        def _():
                            send_slots(to_z * SIDE + dy - 1)
                    else:
                        send_slots(to_z * SIDE + lax.rem(y + dy, SIDE))

    pl.semaphore_wait(greet, 7 + SLABS - 1)
    for dy in (1, 2, 3):
        signal(ready_sem.at[0], tile=tile_at(0, dy))
    for dy in (1, 2, 3):
        send_slots(tile_at(0, dy))
    pl.semaphore_wait(ready_sem.at[0], 3)
    for dz in (2, -2):
        signal(ready_sem.at[1], tile=tile_at(dz, 0))
    send_near(1)
    send_near(2)

    for load in loads:
        load.wait()
    mask[EDGE : EDGE + ROWS] = 0.2 * wet_in[...].astype(jnp.float32)
    rim_out[0, 32:34] = 0.2 * wet_in[0:RIM].astype(jnp.float32)
    rim_out[1, 32:34] = 0.2 * wet_in[ROWS - RIM : ROWS].astype(jnp.float32)
    for f in range(4):
        for l in range(LEVELS):
            i = f * LEVELS + l
            lam[f, l, EDGE : EDGE + ROWS] = cot[f, l]
            rim_out[0, i * RIM : (i + 1) * RIM] = cot[f, l, 0:RIM]
            rim_out[1, i * RIM : (i + 1) * RIM] = cot[f, l, ROWS - RIM : ROWS]

    left, right = lax.rem(me + TILES - 1, TILES), lax.rem(me + 1, TILES)

    def to_neighbours(outgoing, incoming, send, recv):
        return [
            pltpu.make_async_remote_copy(
                src_ref=outgoing.at[side],
                dst_ref=incoming.at[side],
                send_sem=send.at[side],
                recv_sem=recv.at[side],
                device_id={"tile": to},
                device_id_type=MESH,
            )
            for side, to in ((0, left), (1, right))
        ]

    rims = to_neighbours(rim_out, rim_in, rim_send, rim_recv)
    for copy in rims:
        copy.start()

    pl.semaphore_wait(ready_sem.at[1], 2)
    for dz in (4, -4):
        signal(ready_sem.at[2], tile=tile_at(dz, 0))
    send_near(3)
    send_near(4)
    pl.semaphore_wait(ready_sem.at[2], 2)
    @pl.when((z < RING - 1 - 2) & (z > 1))
    def _():
        send_slots(TILES - 1)

    send_planes(ORDER[:SPLIT])

    for copy in rims:
        copy.wait_recv()
    for side, at in ((0, EDGE + ROWS), (1, EDGE - RIM)):
        mask[at : at + RIM] = rim_in[side, 32:34]
        for f in range(4):
            for l in range(LEVELS):
                i = f * LEVELS + l
                lam[f, l, at : at + RIM] = rim_in[side, i * RIM : (i + 1) * RIM]

    total[...] = jnp.zeros_like(total)

    @pl.loop(0, LEVELS)
    def _(l):
        m = mask[...]
        p = slope_x(m * lam[2, l]) + slope_y(m * lam[3, l])
        drive_p[l] = p
        total[...] += p

    def to_slabs(source, incoming, send, recv):
        for k in range(1, SLABS):
            to = lax.rem(lev + k, SLABS)
            pltpu.make_async_remote_copy(
                src_ref=source((lev + k) // SLABS),
                dst_ref=incoming.at[k - 1],
                send_sem=send,
                recv_sem=recv,
                device_id={"lev": to},
                device_id_type=MESH,
            ).start()

    def whole(ref, sem):
        pltpu.make_async_copy(ref, ref, sem).wait()

    to_slabs(lambda turn: total, totals, total_send, total_recv)

    send_planes(ORDER[SPLIT:])

    whole(totals, total_recv)
    whole(totals, total_send)
    total_above = jnp.zeros((PAD, CELLS), jnp.float32)
    for k in range(1, SLABS):
        total_above += jnp.where(k > lev, totals[k - 1], 0.0)

    def second_step(j, running):
        l = LEVELS - 1 - j
        m = mask[...]
        p = drive_p[l]
        running = running + p
        density = 0.2 * (running - 0.5 * p) * thick[l]
        lt, ls, lu, lv = lam[0, l], lam[1, l], lam[2, l], lam[3, l]
        a, b = m * lt, m * ls
        mul_t[l] = a
        mul_s[l] = b
        for i, x in enumerate((a, b)):
            x = 0.5 * x
            moved[i, l] = after(x)
            moved[i + 2, l] = before(x)
            moved[i + 4, l] = pltpu.roll(x, CELLS - 1, 1)
            moved[i + 6, l] = pltpu.roll(x, 1, 1)
        base_t[l] = lt + scale[l] * laplace(a) - 0.25 * density
        base_s[l] = ls + scale[l] * laplace(b) + 0.75 * density
        base_u[l] = lu - 0.5 * (m * lv)
        base_v[l] = lv + 0.5 * (m * lu)
        bend[l] = 0.1 * density
        return running

    lax.fori_loop(0, LEVELS, second_step, total_above)

    own.wait()
    arrived = slots.at[pl.ds(0, (TILES - 1) * SLOTS)]
    whole(arrived, slot_recv)

    field = LEVELS * PAD
    for l in range(LEVELS):
        for r in range(HALO):
            halo_out[0, l * HALO + r] = slots[place[l, r]]
            halo_out[1, l * HALO + r] = slots[place[l, ROWS - HALO + r]]
    halos = to_neighbours(halo_out, halo_in, halo_send, halo_recv)
    for copy in halos:
        copy.start()

    for l in range(LEVELS):

        @pl.loop(0, ROWS // 8)
        def _(g):
            for r in range(8):
                at = l * PAD + EDGE + g * 8 + r
                state[pl.ds(at, 4, stride=field), :] = slots[place[l, g * 8 + r]]

    def start_field(f, l):
        return state[pl.ds(pl.multiple_of(f * field + l * PAD, 8), PAD), :]

    def first_step(l, cut):
        m = cut(mask[...])
        t, s, u, v = (cut(start_field(f, l)) for f in range(4))
        tx, ty, tl = stencil(t)
        sx, sy, sl = stencil(s)
        t1 = t + m * (scale[l] * tl - u * tx - v * ty)
        s1 = s + m * (scale[l] * sl - u * sx - v * sy)
        q = (-0.25 * t + 0.75 * s - 0.05 * t * t) * thick[l]
        a, b = cut(mul_t[l]), cut(mul_s[l])
        mu = cut(base_u[l]) - a * slope_x(t1) - b * slope_x(s1)
        mv = cut(base_v[l]) - a * slope_y(t1) - b * slope_y(s1)
        c, d = m * mu, m * mv
        p = slope_x(c) + slope_y(d)
        return q, t1, tx, ty, sx, sy, mu - 0.5 * d, mv + 0.5 * c, p

    kept = (
        layer, heat, grad.at[0], grad.at[1], grad.at[2], grad.at[3], push_u, push_v, drive_p,
    )

    mid[...] = jnp.zeros_like(mid)

    @pl.loop(0, LEVELS)
    def _(l):
        values = first_step(l, lambda x: x)
        for ref, value in zip(kept, values):
            ref[l] = value
        mid[0] += values[0][8 : PAD - 8]
        mid[1] += values[-1][8 : PAD - 8]

    to_slabs(lambda turn: mid.at[turn], mids, mid_send, mid_recv)

    for copy in halos:
        copy.wait_recv()
    for side, at in ((0, EDGE + ROWS), (1, EDGE - HALO)):
        for l in range(LEVELS):
            for r in range(HALO):
                state[pl.ds(l * PAD + at + r, 4, stride=field), :] = halo_in[side, l * HALO + r]

    found = [
        first_step(l, lambda x: jnp.concatenate([x[:16], x[PAD - 16 :]], 0)) for l in range(LEVELS)
    ]
    for side, sums in ((0, sum(v[0] for v in found)), (1, sum(v[-1] for v in found))):
        edge[side, :8] = sums[:8]
        edge[side, 8:] = sums[24:]

    to_slabs(lambda turn: edge.at[turn], edges, edge_send, edge_recv)
    for l in range(LEVELS):
        for ref, value in zip(kept, found[l]):
            ref[l, :8] = value[:8]
            ref[l, PAD - 8 :] = value[24:]

    def inner(l, running):
        m = mask[...]
        q = layer[l]
        running = running + q
        pressure = 0.2 * (running - 0.5 * q)
        u, v = start_field(2, l), start_field(3, l)
        u1 = u + m * (0.5 * v - slope_x(pressure))
        v1 = v - m * (0.5 * u + slope_y(pressure))
        a, b = mul_t[l], mul_s[l]
        later_t[l] = base_t[l] - bend[l] * heat[l] + slope_x(a * u1) + slope_y(a * v1)
        later_s[l] = base_s[l] + slope_x(b * u1) + slope_y(b * v1)
        return running

    lax.fori_loop(0, LEVELS, inner, jnp.zeros((PAD, CELLS), jnp.float32))

    def upward(j, running):
        l = LEVELS - 1 - j
        p = drive_p[l]
        running = running + p
        adj_q[l] = running - 0.5 * p
        return running

    lax.fori_loop(0, LEVELS, upward, jnp.zeros((PAD, CELLS), jnp.float32))

    def gather_totals(came):
        upper = jnp.zeros(came.shape[1:], jnp.float32)
        lower = jnp.zeros(came.shape[1:], jnp.float32)
        for k in range(1, SLABS):
            upper += jnp.where(k <= lev, came[k - 1], 0.0)
            lower += jnp.where(k > lev, came[k - 1], 0.0)
        return upper, lower

    whole(mids, mid_recv)
    for i, value in enumerate(gather_totals(mids)):
        both[i, 8 : PAD - 8] = value
    whole(edges, edge_recv)
    for i, value in enumerate(gather_totals(edges)):
        both[i, :8] = value[:8]
        both[i, PAD - 8 :] = value[8:]
    m, upper = mask[...], both[0]
    gx, gy = 0.2 * m * slope_x(upper), 0.2 * m * slope_y(upper)
    totals[0] = after(gx)
    totals[1] = before(gx)
    totals[2] = pltpu.roll(gy, CELLS - 1, 1)
    totals[3] = pltpu.roll(gy, 1, 1)

    def spread(x, u, v, k):
        near, along, across = k * x, 0.5 * (x * u), 0.5 * (x * v)
        rows = after(near + along) + before(near - along)
        cells = pltpu.roll(near + across, CELLS - 1, 1) + pltpu.roll(near - across, 1, 1)
        return rows + cells - 4.0 * near

    @pl.loop(0, LEVELS, unroll=UNROLL)
    def _(l):
        m = mask[...]

        def carried(i):
            down, up = moved[i, l] * totals[0], moved[i + 2, l] * totals[1]
            right, left = moved[i + 4, l] * totals[2], moved[i + 6, l] * totals[3]
            return (down - up) + (right - left)

        mt = later_t[l] - carried(0)
        ms = later_s[l] - carried(1)
        a, b = m * mt, m * ms
        t, u, v = start_field(0, l), start_field(2, l), start_field(3, l)
        density = 0.2 * (adj_q[l] + both[1]) * thick[l]
        here = slice(EDGE, EDGE + ROWS)
        out_t = mt + spread(a, u, v, scale[l]) - density * (0.25 + 0.1 * t)
        out_s = ms + spread(b, u, v, scale[l]) + 0.75 * density
        out_u = push_u[l] - a * grad[0, l] - b * grad[2, l]
        out_v = push_v[l] - a * grad[1, l] - b * grad[3, l]
        out[0, l] = out_t[here]
        out[1, l] = out_s[here]
        out[2, l] = out_u[here]
        out[3, l] = out_v[here]

    for copy in rims + halos:
        copy.wait_send()
    whole(arrived, slot_send)
    whole(mids, mid_send)
    whole(edges, edge_send)


def per_device(store, placement, wet, kappa, thickness, cotangent):
    padded = pltpu.VMEM((LEVELS, PAD, CELLS), jnp.float32)
    plane = pltpu.VMEM((PAD, CELLS), jnp.float32)
    planes = pltpu.VMEM((SLABS - 1, PAD, CELLS), jnp.float32)
    dma = pltpu.SemaphoreType.DMA
    scratch = [
        pltpu.VMEM((TILES * SLOTS, 4, CELLS), jnp.float32),
        pltpu.VMEM((4 * LEVELS * PAD, CELLS), jnp.float32),
        pltpu.VMEM((2, LEVELS * HALO, 4, CELLS), jnp.float32),
        pltpu.VMEM((2, LEVELS * HALO, 4, CELLS), jnp.float32),
        pltpu.SMEM((LEVELS, ROWS), jnp.int32),
        pltpu.VMEM((ROWS, CELLS), jnp.int32),
        pltpu.SMEM((LEVELS,), jnp.float32),
        pltpu.SMEM((LEVELS,), jnp.float32),
        pltpu.VMEM((4, LEVELS, ROWS, CELLS), jnp.float32),
        pltpu.VMEM((2, 40, CELLS), jnp.float32),
        pltpu.VMEM((2, 40, CELLS), jnp.float32),
        pltpu.VMEM((4, LEVELS, PAD, CELLS), jnp.float32),
        plane,
        plane,
        planes,
        pltpu.VMEM((2, PAD, CELLS), jnp.float32),
        pltpu.VMEM((2, PAD - 16, CELLS), jnp.float32),
        pltpu.VMEM((SLABS - 1, PAD - 16, CELLS), jnp.float32),
        pltpu.VMEM((2, 16, CELLS), jnp.float32),
        pltpu.VMEM((SLABS - 1, 16, CELLS), jnp.float32),
        padded, padded, padded, padded, padded, padded, padded, padded,
        padded, padded, padded, padded,
        pltpu.VMEM((4, LEVELS, PAD, CELLS), jnp.float32),
        padded, padded, padded,
        pltpu.VMEM((8, LEVELS, PAD, CELLS), jnp.float32),
        dma((5,)),
        pltpu.SemaphoreType.REGULAR((3,)),
        dma, dma, dma,
        dma((2,)), dma((2,)), dma((2,)), dma((2,)),
        dma, dma, dma, dma, dma, dma,
    ]
    return pl.pallas_call(
        kernel,
        out_shape=jax.ShapeDtypeStruct(cotangent.shape, jnp.float32),
        in_specs=[pl.BlockSpec(memory_space=pltpu.HBM)] * 6,
        out_specs=pl.BlockSpec(memory_space=pltpu.VMEM),
        scratch_shapes=scratch,
        compiler_params=pltpu.CompilerParams(
            collective_id=0, has_side_effects=True, vmem_limit_bytes=32 << 20
        ),
    )(
        *[
            pltpu.with_memory_space_constraint(x, pltpu.HBM)
            for x in (
                store.reshape(TILES * SLOTS, 4, CELLS), placement, wet, kappa, thickness, cotangent,
            )
        ]
    )


def solution(mesh):
    placed = (
        P("lev", "tile", None, None, None),
        P("lev", "tile"),
        P("tile", None),
        P("lev"),
        P("lev"),
        P(None, "lev", "tile", None),
    )
    return jax.shard_map(
        per_device,
        mesh=mesh,
        in_specs=placed,
        out_specs=P(None, "lev", "tile", None),
        check_vma=False,
    )
```

```python
import functools

import jax
import jax.numpy as jnp
from jax import lax
from jax.experimental import pallas as pl
from jax.experimental.pallas import tpu as pltpu
from jax.sharding import PartitionSpec as P

MESH = pl.DeviceIdType.MESH
LEVELS = 4
ROWS = 64
CELLS = 128
PAD = 72
EDGE = 4
SLOTS = 8
TILES = 64
RING = 16
SIDE = 4
SLABS = 8
HALO = 3
EARLY = (0, 1)
ORDER = (0, 1, 2, 3, 4, 5, 6, 15, 7, 14, 13, 8, 12, 9, 10, 11)
SPLIT = 5
NEAR = 4
UNROLL = True
RIM = 2


def before(x):
    return pltpu.roll(x, 1, 0)


def after(x):
    return pltpu.roll(x, x.shape[0] - 1, 0)


def slope_x(x):
    return 0.5 * (after(x) - before(x))


def slope_y(x):
    return 0.5 * (pltpu.roll(x, CELLS - 1, 1) - pltpu.roll(x, 1, 1))


def stencil(x):
    down, up = after(x), before(x)
    right, left = pltpu.roll(x, CELLS - 1, 1), pltpu.roll(x, 1, 1)
    return 0.5 * (down - up), 0.5 * (right - left), (down + up) + (right + left) - 4.0 * x


def laplace(x):
    return stencil(x)[2]


def kernel(
    store, placement, wet, kappa, thickness, cotangent, out,
    slots, state, halo_out, halo_in, place, wet_in, scale, thick, cot, rim_out, rim_in,
    lam, mask, total, totals, both, mid, mids, edge, edges,
    drive_p, mul_t, mul_s, base_t, base_s, base_u, base_v, bend,
    heat, layer, push_u, push_v, grad, later_t, later_s, adj_q, moved,
    load_sem, ready_sem, slot_send, slot_recv, own_sem, halo_send, halo_recv,
    rim_send, rim_recv, total_send, total_recv, mid_send, mid_recv, edge_send, edge_recv,
):
    me = lax.axis_index("tile")
    lev = lax.axis_index("lev")
    z, y = me // SIDE, lax.rem(me, SIDE)

    def tile_at(dz, dy):
        return lax.rem(z + (dz + RING), RING) * SIDE + lax.rem(y + dy, SIDE)

    def signal(sem, **where):
        pl.semaphore_signal(sem, inc=1, device_id=where, device_id_type=MESH)

    greet = pltpu.get_barrier_semaphore()
    for dz in (1, -1, 2, -2):
        signal(greet, tile=tile_at(dz, 0))
    for dy in (1, 2, 3):
        signal(greet, tile=tile_at(0, dy))
    for k in range(1, SLABS):
        signal(greet, lev=lax.rem(lev + k, SLABS))

    loads = [
        pltpu.make_async_copy(cotangent, cot, load_sem.at[0]),
        pltpu.make_async_copy(wet, wet_in, load_sem.at[1]),
        pltpu.make_async_copy(placement, place, load_sem.at[2]),
        pltpu.make_async_copy(kappa, scale, load_sem.at[3]),
        pltpu.make_async_copy(thickness, thick, load_sem.at[4]),
    ]
    for load in loads:
        load.start()

    def is_early(plane):
        return functools.reduce(lambda found, e: found | (plane == e), EARLY, plane < 0)

    own = pltpu.make_async_copy(
        store.at[pl.ds(me * SLOTS, SLOTS)], slots.at[pl.ds(me * SLOTS, SLOTS)], own_sem
    )
    own.start()

    def send_slots(to):
        pltpu.make_async_remote_copy(
            src_ref=store.at[pl.ds(to * SLOTS, SLOTS)],
            dst_ref=slots.at[pl.ds(me * SLOTS, SLOTS)],
            send_sem=slot_send,
            recv_sem=slot_recv,
            device_id={"tile": to},
            device_id_type=MESH,
        ).start()

    def send_near(reach):
        for dz in (reach, -reach):
            to_z = lax.rem(z + (dz + RING), RING)

            @pl.when(is_early(to_z) if reach > 2 else z >= 0)
            def _():
                @pl.loop(0, SIDE)
                def _(dy):
                    send_slots(tile_at(dz, dy))

    def send_planes(planes):
        for to_z in planes:
            gap = lax.rem(z + (RING - to_z), RING)
            gap = jnp.minimum(gap, RING - gap)

            @pl.when(gap > (NEAR if to_z in EARLY else 2))
            def _():
                @pl.loop(0, SIDE)
                def _(dy):
                    if to_z == RING - 1:

                        @pl.when(dy > 0)
                        def _():
                            send_slots(to_z * SIDE + dy - 1)
                    else:
                        send_slots(to_z * SIDE + lax.rem(y + dy, SIDE))

    pl.semaphore_wait(greet, 7 + SLABS - 1)
    for dy in (1, 2, 3):
        signal(ready_sem.at[0], tile=tile_at(0, dy))
    for dy in (1, 2, 3):
        send_slots(tile_at(0, dy))
    pl.semaphore_wait(ready_sem.at[0], 3)
    for dz in (2, -2):
        signal(ready_sem.at[1], tile=tile_at(dz, 0))
    send_near(1)
    send_near(2)

    for load in loads:
        load.wait()
    mask[EDGE : EDGE + ROWS] = 0.2 * wet_in[...].astype(jnp.float32)
    rim_out[0, 32:34] = 0.2 * wet_in[0:RIM].astype(jnp.float32)
    rim_out[1, 32:34] = 0.2 * wet_in[ROWS - RIM : ROWS].astype(jnp.float32)
    for f in range(4):
        for l in range(LEVELS):
            i = f * LEVELS + l
            lam[f, l, EDGE : EDGE + ROWS] = cot[f, l]
            rim_out[0, i * RIM : (i + 1) * RIM] = cot[f, l, 0:RIM]
            rim_out[1, i * RIM : (i + 1) * RIM] = cot[f, l, ROWS - RIM : ROWS]

    left, right = lax.rem(me + TILES - 1, TILES), lax.rem(me + 1, TILES)

    def to_neighbours(outgoing, incoming, send, recv):
        return [
            pltpu.make_async_remote_copy(
                src_ref=outgoing.at[side],
                dst_ref=incoming.at[side],
                send_sem=send.at[side],
                recv_sem=recv.at[side],
                device_id={"tile": to},
                device_id_type=MESH,
            )
            for side, to in ((0, left), (1, right))
        ]

    rims = to_neighbours(rim_out, rim_in, rim_send, rim_recv)
    for copy in rims:
        copy.start()

    pl.semaphore_wait(ready_sem.at[1], 2)
    for dz in (4, -4):
        signal(ready_sem.at[2], tile=tile_at(dz, 0))
    send_near(3)
    send_near(4)
    pl.semaphore_wait(ready_sem.at[2], 2)
    @pl.when((z < RING - 1 - 2) & (z > 1))
    def _():
        send_slots(TILES - 1)

    send_planes(ORDER[:SPLIT])

    for copy in rims:
        copy.wait_recv()
    for side, at in ((0, EDGE + ROWS), (1, EDGE - RIM)):
        mask[at : at + RIM] = rim_in[side, 32:34]
        for f in range(4):
            for l in range(LEVELS):
                i = f * LEVELS + l
                lam[f, l, at : at + RIM] = rim_in[side, i * RIM : (i + 1) * RIM]

    total[...] = jnp.zeros_like(total)

    @pl.loop(0, LEVELS)
    def _(l):
        m = mask[...]
        p = slope_x(m * lam[2, l]) + slope_y(m * lam[3, l])
        drive_p[l] = p
        total[...] += p

    def to_slabs(source, incoming, send, recv):
        for k in (4, 3, 5, 2, 6, 1, 7):
            to = lax.rem(lev + k, SLABS)
            pltpu.make_async_remote_copy(
                src_ref=source((lev + k) // SLABS),
                dst_ref=incoming.at[k - 1],
                send_sem=send,
                recv_sem=recv,
                device_id={"lev": to},
                device_id_type=MESH,
            ).start()

    def whole(ref, sem):
        pltpu.make_async_copy(ref, ref, sem).wait()

    to_slabs(lambda turn: total, totals, total_send, total_recv)

    send_planes(ORDER[SPLIT:])

    whole(totals, total_recv)
    whole(totals, total_send)
    total_above = jnp.zeros((PAD, CELLS), jnp.float32)
    for k in range(1, SLABS):
        total_above += jnp.where(k > lev, totals[k - 1], 0.0)

    def second_step(j, running):
        l = LEVELS - 1 - j
        m = mask[...]
        p = drive_p[l]
        running = running + p
        density = 0.2 * (running - 0.5 * p) * thick[l]
        lt, ls, lu, lv = lam[0, l], lam[1, l], lam[2, l], lam[3, l]
        a, b = m * lt, m * ls
        mul_t[l] = a
        mul_s[l] = b
        for i, x in enumerate((a, b)):
            x = 0.5 * x
            moved[i, l] = after(x)
            moved[i + 2, l] = before(x)
            moved[i + 4, l] = pltpu.roll(x, CELLS - 1, 1)
            moved[i + 6, l] = pltpu.roll(x, 1, 1)
        base_t[l] = lt + scale[l] * laplace(a) - 0.25 * density
        base_s[l] = ls + scale[l] * laplace(b) + 0.75 * density
        base_u[l] = lu - 0.5 * (m * lv)
        base_v[l] = lv + 0.5 * (m * lu)
        bend[l] = 0.1 * density
        return running

    lax.fori_loop(0, LEVELS, second_step, total_above)

    own.wait()
    arrived = slots.at[pl.ds(0, (TILES - 1) * SLOTS)]
    whole(arrived, slot_recv)

    field = LEVELS * PAD
    halos = to_neighbours(halo_out, halo_in, halo_send, halo_recv)
    for side, first in ((1, ROWS - HALO), (0, 0)):
        for l in range(LEVELS):
            for r in range(HALO):
                halo_out[side, l * HALO + r] = slots[place[l, first + r]]
        halos[side].start()

    for l in range(LEVELS):

        @pl.loop(0, ROWS // 8)
        def _(g):
            for r in range(8):
                at = l * PAD + EDGE + g * 8 + r
                state[pl.ds(at, 4, stride=field), :] = slots[place[l, g * 8 + r]]

    def start_field(f, l):
        return state[pl.ds(pl.multiple_of(f * field + l * PAD, 8), PAD), :]

    def first_step(l, cut):
        m = cut(mask[...])
        t, s, u, v = (cut(start_field(f, l)) for f in range(4))
        tx, ty, tl = stencil(t)
        sx, sy, sl = stencil(s)
        t1 = t + m * (scale[l] * tl - u * tx - v * ty)
        s1 = s + m * (scale[l] * sl - u * sx - v * sy)
        q = (-0.25 * t + 0.75 * s - 0.05 * t * t) * thick[l]
        a, b = cut(mul_t[l]), cut(mul_s[l])
        mu = cut(base_u[l]) - a * slope_x(t1) - b * slope_x(s1)
        mv = cut(base_v[l]) - a * slope_y(t1) - b * slope_y(s1)
        c, d = m * mu, m * mv
        p = slope_x(c) + slope_y(d)
        return q, t1, tx, ty, sx, sy, mu - 0.5 * d, mv + 0.5 * c, p

    kept = (
        layer, heat, grad.at[0], grad.at[1], grad.at[2], grad.at[3], push_u, push_v, drive_p,
    )

    mid[...] = jnp.zeros_like(mid)

    @pl.loop(0, LEVELS)
    def _(l):
        values = first_step(l, lambda x: x)
        for ref, value in zip(kept, values):
            ref[l] = value
        mid[0] += values[0][8 : PAD - 8]
        mid[1] += values[-1][8 : PAD - 8]

    to_slabs(lambda turn: mid.at[turn], mids, mid_send, mid_recv)

    for copy in halos:
        copy.wait_recv()
    for side, at in ((0, EDGE + ROWS), (1, EDGE - HALO)):
        for l in range(LEVELS):
            for r in range(HALO):
                state[pl.ds(l * PAD + at + r, 4, stride=field), :] = halo_in[side, l * HALO + r]

    found = [
        first_step(l, lambda x: jnp.concatenate([x[:16], x[PAD - 16 :]], 0)) for l in range(LEVELS)
    ]
    for side, sums in ((0, sum(v[0] for v in found)), (1, sum(v[-1] for v in found))):
        edge[side, :8] = sums[:8]
        edge[side, 8:] = sums[24:]

    to_slabs(lambda turn: edge.at[turn], edges, edge_send, edge_recv)
    for l in range(LEVELS):
        for ref, value in zip(kept, found[l]):
            ref[l, :8] = value[:8]
            ref[l, PAD - 8 :] = value[24:]

    def inner(l, running):
        m = mask[...]
        q = layer[l]
        running = running + q
        pressure = 0.2 * (running - 0.5 * q)
        u, v = start_field(2, l), start_field(3, l)
        u1 = u + m * (0.5 * v - slope_x(pressure))
        v1 = v - m * (0.5 * u + slope_y(pressure))
        a, b = mul_t[l], mul_s[l]
        later_t[l] = base_t[l] - bend[l] * heat[l] + slope_x(a * u1) + slope_y(a * v1)
        later_s[l] = base_s[l] + slope_x(b * u1) + slope_y(b * v1)
        return running

    lax.fori_loop(0, LEVELS, inner, jnp.zeros((PAD, CELLS), jnp.float32))

    def upward(j, running):
        l = LEVELS - 1 - j
        p = drive_p[l]
        running = running + p
        adj_q[l] = running - 0.5 * p
        return running

    lax.fori_loop(0, LEVELS, upward, jnp.zeros((PAD, CELLS), jnp.float32))

    def gather_totals(came):
        upper = jnp.zeros(came.shape[1:], jnp.float32)
        lower = jnp.zeros(came.shape[1:], jnp.float32)
        for k in range(1, SLABS):
            upper += jnp.where(k <= lev, came[k - 1], 0.0)
            lower += jnp.where(k > lev, came[k - 1], 0.0)
        return upper, lower

    whole(mids, mid_recv)
    for i, value in enumerate(gather_totals(mids)):
        both[i, 8 : PAD - 8] = value
    whole(edges, edge_recv)
    for i, value in enumerate(gather_totals(edges)):
        both[i, :8] = value[:8]
        both[i, PAD - 8 :] = value[8:]
    m, upper = mask[...], both[0]
    gx, gy = 0.2 * m * slope_x(upper), 0.2 * m * slope_y(upper)
    totals[0] = after(gx)
    totals[1] = before(gx)
    totals[2] = pltpu.roll(gy, CELLS - 1, 1)
    totals[3] = pltpu.roll(gy, 1, 1)

    def spread(x, u, v, k):
        near, along, across = k * x, 0.5 * (x * u), 0.5 * (x * v)
        rows = after(near + along) + before(near - along)
        cells = pltpu.roll(near + across, CELLS - 1, 1) + pltpu.roll(near - across, 1, 1)
        return rows + cells - 4.0 * near

    @pl.loop(0, LEVELS, unroll=UNROLL)
    def _(l):
        m = mask[...]

        def carried(i):
            down, up = moved[i, l] * totals[0], moved[i + 2, l] * totals[1]
            right, left = moved[i + 4, l] * totals[2], moved[i + 6, l] * totals[3]
            return (down - up) + (right - left)

        mt = later_t[l] - carried(0)
        ms = later_s[l] - carried(1)
        a, b = m * mt, m * ms
        t, u, v = start_field(0, l), start_field(2, l), start_field(3, l)
        density = 0.2 * (adj_q[l] + both[1]) * thick[l]
        here = slice(EDGE, EDGE + ROWS)
        out_t = mt + spread(a, u, v, scale[l]) - density * (0.25 + 0.1 * t)
        out_s = ms + spread(b, u, v, scale[l]) + 0.75 * density
        out_u = push_u[l] - a * grad[0, l] - b * grad[2, l]
        out_v = push_v[l] - a * grad[1, l] - b * grad[3, l]
        out[0, l] = out_t[here]
        out[1, l] = out_s[here]
        out[2, l] = out_u[here]
        out[3, l] = out_v[here]

    for copy in rims + halos:
        copy.wait_send()
    whole(arrived, slot_send)
    whole(mids, mid_send)
    whole(edges, edge_send)


def per_device(store, placement, wet, kappa, thickness, cotangent):
    padded = pltpu.VMEM((LEVELS, PAD, CELLS), jnp.float32)
    plane = pltpu.VMEM((PAD, CELLS), jnp.float32)
    planes = pltpu.VMEM((SLABS - 1, PAD, CELLS), jnp.float32)
    dma = pltpu.SemaphoreType.DMA
    scratch = [
        pltpu.VMEM((TILES * SLOTS, 4, CELLS), jnp.float32),
        pltpu.VMEM((4 * LEVELS * PAD, CELLS), jnp.float32),
        pltpu.VMEM((2, LEVELS * HALO, 4, CELLS), jnp.float32),
        pltpu.VMEM((2, LEVELS * HALO, 4, CELLS), jnp.float32),
        pltpu.SMEM((LEVELS, ROWS), jnp.int32),
        pltpu.VMEM((ROWS, CELLS), jnp.int32),
        pltpu.SMEM((LEVELS,), jnp.float32),
        pltpu.SMEM((LEVELS,), jnp.float32),
        pltpu.VMEM((4, LEVELS, ROWS, CELLS), jnp.float32),
        pltpu.VMEM((2, 40, CELLS), jnp.float32),
        pltpu.VMEM((2, 40, CELLS), jnp.float32),
        pltpu.VMEM((4, LEVELS, PAD, CELLS), jnp.float32),
        plane,
        plane,
        planes,
        pltpu.VMEM((2, PAD, CELLS), jnp.float32),
        pltpu.VMEM((2, PAD - 16, CELLS), jnp.float32),
        pltpu.VMEM((SLABS - 1, PAD - 16, CELLS), jnp.float32),
        pltpu.VMEM((2, 16, CELLS), jnp.float32),
        pltpu.VMEM((SLABS - 1, 16, CELLS), jnp.float32),
        padded, padded, padded, padded, padded, padded, padded, padded,
        padded, padded, padded, padded,
        pltpu.VMEM((4, LEVELS, PAD, CELLS), jnp.float32),
        padded, padded, padded,
        pltpu.VMEM((8, LEVELS, PAD, CELLS), jnp.float32),
        dma((5,)),
        pltpu.SemaphoreType.REGULAR((3,)),
        dma, dma, dma,
        dma((2,)), dma((2,)), dma((2,)), dma((2,)),
        dma, dma, dma, dma, dma, dma,
    ]
    return pl.pallas_call(
        kernel,
        out_shape=jax.ShapeDtypeStruct(cotangent.shape, jnp.float32),
        in_specs=[pl.BlockSpec(memory_space=pltpu.HBM)] * 6,
        out_specs=pl.BlockSpec(memory_space=pltpu.VMEM),
        scratch_shapes=scratch,
        compiler_params=pltpu.CompilerParams(
            collective_id=0, has_side_effects=True, vmem_limit_bytes=32 << 20
        ),
    )(
        *[
            pltpu.with_memory_space_constraint(x, pltpu.HBM)
            for x in (
                store.reshape(TILES * SLOTS, 4, CELLS), placement, wet, kappa, thickness, cotangent,
            )
        ]
    )


def solution(mesh):
    placed = (
        P("lev", "tile", None, None, None),
        P("lev", "tile"),
        P("tile", None),
        P("lev"),
        P("lev"),
        P(None, "lev", "tile", None),
    )
    return jax.shard_map(
        per_device,
        mesh=mesh,
        in_specs=placed,
        out_specs=P(None, "lev", "tile", None),
        check_vma=False,
    )
```

```python
import functools

import jax
import jax.numpy as jnp
from jax import lax
from jax.experimental import pallas as pl
from jax.experimental.pallas import tpu as pltpu
from jax.sharding import PartitionSpec as P

MESH = pl.DeviceIdType.MESH
LEVELS = 4
ROWS = 64
CELLS = 128
PAD = 72
EDGE = 4
SLOTS = 8
TILES = 64
RING = 16
SIDE = 4
SLABS = 8
HALO = 3
EARLY = (0, 1)
ORDER = (0, 1, 2, 3, 4, 5, 6, 15, 7, 14, 13, 8, 12, 9, 10, 11)
SPLIT = 5
NEAR = 4
UNROLL = True
RIM = 2


def before(x):
    return pltpu.roll(x, 1, 0)


def after(x):
    return pltpu.roll(x, x.shape[0] - 1, 0)


def slope_x(x):
    return 0.5 * (after(x) - before(x))


def slope_y(x):
    return 0.5 * (pltpu.roll(x, CELLS - 1, 1) - pltpu.roll(x, 1, 1))


def stencil(x):
    down, up = after(x), before(x)
    right, left = pltpu.roll(x, CELLS - 1, 1), pltpu.roll(x, 1, 1)
    return 0.5 * (down - up), 0.5 * (right - left), (down + up) + (right + left) - 4.0 * x


def laplace(x):
    return stencil(x)[2]


def kernel(
    store, placement, wet, kappa, thickness, cotangent, out,
    slots, state, halo_out, halo_in, place, wet_in, scale, thick, cot, rim_out, rim_in,
    lam, mask, total, totals, both, mid, mids, edge, edges,
    drive_p, mul_t, mul_s, base_t, base_s, base_u, base_v, bend,
    heat, layer, push_u, push_v, grad, later_t, later_s, adj_q, moved,
    load_sem, ready_sem, slot_send, slot_recv, own_sem, halo_send, halo_recv,
    rim_send, rim_recv, total_send, total_recv, mid_send, mid_recv, edge_send, edge_recv,
):
    me = lax.axis_index("tile")
    lev = lax.axis_index("lev")
    z, y = me // SIDE, lax.rem(me, SIDE)

    def tile_at(dz, dy):
        return lax.rem(z + (dz + RING), RING) * SIDE + lax.rem(y + dy, SIDE)

    def signal(sem, **where):
        pl.semaphore_signal(sem, inc=1, device_id=where, device_id_type=MESH)

    greet = pltpu.get_barrier_semaphore()
    for dz in (1, -1, 2, -2):
        signal(greet, tile=tile_at(dz, 0))
    for dy in (1, 2, 3):
        signal(greet, tile=tile_at(0, dy))
    def nearest_slabs(sem):
        signal(sem, lev=lev + 1 - 2 * lax.rem(lev, 2))
        for k in (2, 4, 6):
            signal(sem, lev=lax.rem(lev + k, SLABS))

    nearest_slabs(greet)

    loads = [
        pltpu.make_async_copy(cotangent, cot, load_sem.at[0]),
        pltpu.make_async_copy(wet, wet_in, load_sem.at[1]),
        pltpu.make_async_copy(placement, place, load_sem.at[2]),
        pltpu.make_async_copy(kappa, scale, load_sem.at[3]),
        pltpu.make_async_copy(thickness, thick, load_sem.at[4]),
    ]
    for load in loads:
        load.start()

    def is_early(plane):
        return functools.reduce(lambda found, e: found | (plane == e), EARLY, plane < 0)

    own = pltpu.make_async_copy(
        store.at[pl.ds(me * SLOTS, SLOTS)], slots.at[pl.ds(me * SLOTS, SLOTS)], own_sem
    )
    own.start()

    def send_slots(to):
        pltpu.make_async_remote_copy(
            src_ref=store.at[pl.ds(to * SLOTS, SLOTS)],
            dst_ref=slots.at[pl.ds(me * SLOTS, SLOTS)],
            send_sem=slot_send,
            recv_sem=slot_recv,
            device_id={"tile": to},
            device_id_type=MESH,
        ).start()

    def send_near(reach):
        for dz in (reach, -reach):
            to_z = lax.rem(z + (dz + RING), RING)

            @pl.when(is_early(to_z) if reach > 2 else z >= 0)
            def _():
                @pl.loop(0 if reach > 2 else 1, SIDE)
                def _(dy):
                    send_slots(tile_at(dz, dy))

    def send_planes(planes):
        for to_z in planes:
            gap = lax.rem(z + (RING - to_z), RING)
            gap = jnp.minimum(gap, RING - gap)

            @pl.when(gap > (NEAR if to_z in EARLY else 2))
            def _():
                @pl.loop(0, SIDE)
                def _(dy):
                    if to_z == RING - 1:

                        @pl.when(dy > 0)
                        def _():
                            send_slots(to_z * SIDE + dy - 1)
                    else:
                        send_slots(to_z * SIDE + lax.rem(y + dy, SIDE))

    pl.semaphore_wait(greet, 7 + 4)
    for dy in (1, 2, 3):
        signal(ready_sem.at[0], tile=tile_at(0, dy))
    for dz in (1, -1, 2, -2):
        send_slots(tile_at(dz, 0))
    for dy in (1, 2, 3):
        send_slots(tile_at(0, dy))
    nearest_slabs(ready_sem.at[3])
    pl.semaphore_wait(ready_sem.at[0], 3)
    for dz in (2, -2):
        signal(ready_sem.at[1], tile=tile_at(dz, 0))
    send_near(1)
    send_near(2)

    for load in loads:
        load.wait()
    mask[EDGE : EDGE + ROWS] = 0.2 * wet_in[...].astype(jnp.float32)
    rim_out[0, 32:34] = 0.2 * wet_in[0:RIM].astype(jnp.float32)
    rim_out[1, 32:34] = 0.2 * wet_in[ROWS - RIM : ROWS].astype(jnp.float32)
    for f in range(4):
        for l in range(LEVELS):
            i = f * LEVELS + l
            lam[f, l, EDGE : EDGE + ROWS] = cot[f, l]
            rim_out[0, i * RIM : (i + 1) * RIM] = cot[f, l, 0:RIM]
            rim_out[1, i * RIM : (i + 1) * RIM] = cot[f, l, ROWS - RIM : ROWS]

    left, right = lax.rem(me + TILES - 1, TILES), lax.rem(me + 1, TILES)

    def to_neighbours(outgoing, incoming, send, recv):
        return [
            pltpu.make_async_remote_copy(
                src_ref=outgoing.at[side],
                dst_ref=incoming.at[side],
                send_sem=send.at[side],
                recv_sem=recv.at[side],
                device_id={"tile": to},
                device_id_type=MESH,
            )
            for side, to in ((0, left), (1, right))
        ]

    rims = to_neighbours(rim_out, rim_in, rim_send, rim_recv)
    for copy in rims:
        copy.start()

    pl.semaphore_wait(ready_sem.at[1], 2)
    for dz in (4, -4):
        signal(ready_sem.at[2], tile=tile_at(dz, 0))
    send_near(3)
    send_near(4)
    pl.semaphore_wait(ready_sem.at[2], 2)
    @pl.when((z < RING - 1 - 2) & (z > 1))
    def _():
        send_slots(TILES - 1)

    send_planes(ORDER[:SPLIT])

    for copy in rims:
        copy.wait_recv()
    for side, at in ((0, EDGE + ROWS), (1, EDGE - RIM)):
        mask[at : at + RIM] = rim_in[side, 32:34]
        for f in range(4):
            for l in range(LEVELS):
                i = f * LEVELS + l
                lam[f, l, at : at + RIM] = rim_in[side, i * RIM : (i + 1) * RIM]

    total[...] = jnp.zeros_like(total)

    @pl.loop(0, LEVELS)
    def _(l):
        m = mask[...]
        p = slope_x(m * lam[2, l]) + slope_y(m * lam[3, l])
        drive_p[l] = p
        total[...] += p

    def to_slabs(source, incoming, send, recv):
        for k in (4, 3, 5, 2, 6, 1, 7):
            to = lax.rem(lev + k, SLABS)
            pltpu.make_async_remote_copy(
                src_ref=source((lev + k) // SLABS),
                dst_ref=incoming.at[k - 1],
                send_sem=send,
                recv_sem=recv,
                device_id={"lev": to},
                device_id_type=MESH,
            ).start()

    def whole(ref, sem):
        pltpu.make_async_copy(ref, ref, sem).wait()

    pl.semaphore_wait(ready_sem.at[3], 4)
    to_slabs(lambda turn: total, totals, total_send, total_recv)

    send_planes(ORDER[SPLIT:])

    whole(totals, total_recv)
    whole(totals, total_send)
    total_above = jnp.zeros((PAD, CELLS), jnp.float32)
    for k in range(1, SLABS):
        total_above += jnp.where(k > lev, totals[k - 1], 0.0)

    def second_step(j, running):
        l = LEVELS - 1 - j
        m = mask[...]
        p = drive_p[l]
        running = running + p
        density = 0.2 * (running - 0.5 * p) * thick[l]
        lt, ls, lu, lv = lam[0, l], lam[1, l], lam[2, l], lam[3, l]
        a, b = m * lt, m * ls
        mul_t[l] = a
        mul_s[l] = b
        for i, x in enumerate((a, b)):
            x = 0.5 * x
            moved[i, l] = after(x)
            moved[i + 2, l] = before(x)
            moved[i + 4, l] = pltpu.roll(x, CELLS - 1, 1)
            moved[i + 6, l] = pltpu.roll(x, 1, 1)
        base_t[l] = lt + scale[l] * laplace(a) - 0.25 * density
        base_s[l] = ls + scale[l] * laplace(b) + 0.75 * density
        base_u[l] = lu - 0.5 * (m * lv)
        base_v[l] = lv + 0.5 * (m * lu)
        bend[l] = 0.1 * density
        return running

    lax.fori_loop(0, LEVELS, second_step, total_above)

    own.wait()
    arrived = slots.at[pl.ds(0, (TILES - 1) * SLOTS)]
    whole(arrived, slot_recv)

    field = LEVELS * PAD
    halos = to_neighbours(halo_out, halo_in, halo_send, halo_recv)
    for side, first in ((1, ROWS - HALO), (0, 0)):
        for l in range(LEVELS):
            for r in range(HALO):
                halo_out[side, l * HALO + r] = slots[place[l, first + r]]
        halos[side].start()

    for l in range(LEVELS):

        @pl.loop(0, ROWS // 8)
        def _(g):
            for r in range(8):
                at = l * PAD + EDGE + g * 8 + r
                state[pl.ds(at, 4, stride=field), :] = slots[place[l, g * 8 + r]]

    def start_field(f, l):
        return state[pl.ds(pl.multiple_of(f * field + l * PAD, 8), PAD), :]

    def first_step(l, cut):
        m = cut(mask[...])
        t, s, u, v = (cut(start_field(f, l)) for f in range(4))
        tx, ty, tl = stencil(t)
        sx, sy, sl = stencil(s)
        t1 = t + m * (scale[l] * tl - u * tx - v * ty)
        s1 = s + m * (scale[l] * sl - u * sx - v * sy)
        q = (-0.25 * t + 0.75 * s - 0.05 * t * t) * thick[l]
        a, b = cut(mul_t[l]), cut(mul_s[l])
        mu = cut(base_u[l]) - a * slope_x(t1) - b * slope_x(s1)
        mv = cut(base_v[l]) - a * slope_y(t1) - b * slope_y(s1)
        c, d = m * mu, m * mv
        p = slope_x(c) + slope_y(d)
        return q, t1, tx, ty, sx, sy, mu - 0.5 * d, mv + 0.5 * c, p

    kept = (
        layer, heat, grad.at[0], grad.at[1], grad.at[2], grad.at[3], push_u, push_v, drive_p,
    )

    mid[...] = jnp.zeros_like(mid)

    @pl.loop(0, LEVELS)
    def _(l):
        values = first_step(l, lambda x: x)
        for ref, value in zip(kept, values):
            ref[l] = value
        mid[0] += values[0][8 : PAD - 8]
        mid[1] += values[-1][8 : PAD - 8]

    to_slabs(lambda turn: mid.at[turn], mids, mid_send, mid_recv)

    for copy in halos:
        copy.wait_recv()
    for side, at in ((0, EDGE + ROWS), (1, EDGE - HALO)):
        for l in range(LEVELS):
            for r in range(HALO):
                state[pl.ds(l * PAD + at + r, 4, stride=field), :] = halo_in[side, l * HALO + r]

    found = [
        first_step(l, lambda x: jnp.concatenate([x[:16], x[PAD - 16 :]], 0)) for l in range(LEVELS)
    ]
    for side, sums in ((0, sum(v[0] for v in found)), (1, sum(v[-1] for v in found))):
        edge[side, :8] = sums[:8]
        edge[side, 8:] = sums[24:]

    to_slabs(lambda turn: edge.at[turn], edges, edge_send, edge_recv)
    for l in range(LEVELS):
        for ref, value in zip(kept, found[l]):
            ref[l, :8] = value[:8]
            ref[l, PAD - 8 :] = value[24:]

    def inner(l, running):
        m = mask[...]
        q = layer[l]
        running = running + q
        pressure = 0.2 * (running - 0.5 * q)
        u, v = start_field(2, l), start_field(3, l)
        u1 = u + m * (0.5 * v - slope_x(pressure))
        v1 = v - m * (0.5 * u + slope_y(pressure))
        a, b = mul_t[l], mul_s[l]
        later_t[l] = base_t[l] - bend[l] * heat[l] + slope_x(a * u1) + slope_y(a * v1)
        later_s[l] = base_s[l] + slope_x(b * u1) + slope_y(b * v1)
        return running

    lax.fori_loop(0, LEVELS, inner, jnp.zeros((PAD, CELLS), jnp.float32))

    def upward(j, running):
        l = LEVELS - 1 - j
        p = drive_p[l]
        running = running + p
        adj_q[l] = running - 0.5 * p
        return running

    lax.fori_loop(0, LEVELS, upward, jnp.zeros((PAD, CELLS), jnp.float32))

    def gather_totals(came):
        upper = jnp.zeros(came.shape[1:], jnp.float32)
        lower = jnp.zeros(came.shape[1:], jnp.float32)
        for k in range(1, SLABS):
            upper += jnp.where(k <= lev, came[k - 1], 0.0)
            lower += jnp.where(k > lev, came[k - 1], 0.0)
        return upper, lower

    whole(mids, mid_recv)
    for i, value in enumerate(gather_totals(mids)):
        both[i, 8 : PAD - 8] = value
    whole(edges, edge_recv)
    for i, value in enumerate(gather_totals(edges)):
        both[i, :8] = value[:8]
        both[i, PAD - 8 :] = value[8:]
    m, upper = mask[...], both[0]
    gx, gy = 0.2 * m * slope_x(upper), 0.2 * m * slope_y(upper)
    totals[0] = after(gx)
    totals[1] = before(gx)
    totals[2] = pltpu.roll(gy, CELLS - 1, 1)
    totals[3] = pltpu.roll(gy, 1, 1)

    def spread(x, u, v, k):
        near, along, across = k * x, 0.5 * (x * u), 0.5 * (x * v)
        rows = after(near + along) + before(near - along)
        cells = pltpu.roll(near + across, CELLS - 1, 1) + pltpu.roll(near - across, 1, 1)
        return rows + cells - 4.0 * near

    @pl.loop(0, LEVELS, unroll=UNROLL)
    def _(l):
        m = mask[...]

        def carried(i):
            down, up = moved[i, l] * totals[0], moved[i + 2, l] * totals[1]
            right, left = moved[i + 4, l] * totals[2], moved[i + 6, l] * totals[3]
            return (down - up) + (right - left)

        mt = later_t[l] - carried(0)
        ms = later_s[l] - carried(1)
        a, b = m * mt, m * ms
        t, u, v = start_field(0, l), start_field(2, l), start_field(3, l)
        density = 0.2 * (adj_q[l] + both[1]) * thick[l]
        here = slice(EDGE, EDGE + ROWS)
        out_t = mt + spread(a, u, v, scale[l]) - density * (0.25 + 0.1 * t)
        out_s = ms + spread(b, u, v, scale[l]) + 0.75 * density
        out_u = push_u[l] - a * grad[0, l] - b * grad[2, l]
        out_v = push_v[l] - a * grad[1, l] - b * grad[3, l]
        out[0, l] = out_t[here]
        out[1, l] = out_s[here]
        out[2, l] = out_u[here]
        out[3, l] = out_v[here]

    for copy in rims + halos:
        copy.wait_send()
    whole(arrived, slot_send)
    whole(mids, mid_send)
    whole(edges, edge_send)


def per_device(store, placement, wet, kappa, thickness, cotangent):
    padded = pltpu.VMEM((LEVELS, PAD, CELLS), jnp.float32)
    plane = pltpu.VMEM((PAD, CELLS), jnp.float32)
    planes = pltpu.VMEM((SLABS - 1, PAD, CELLS), jnp.float32)
    dma = pltpu.SemaphoreType.DMA
    scratch = [
        pltpu.VMEM((TILES * SLOTS, 4, CELLS), jnp.float32),
        pltpu.VMEM((4 * LEVELS * PAD, CELLS), jnp.float32),
        pltpu.VMEM((2, LEVELS * HALO, 4, CELLS), jnp.float32),
        pltpu.VMEM((2, LEVELS * HALO, 4, CELLS), jnp.float32),
        pltpu.SMEM((LEVELS, ROWS), jnp.int32),
        pltpu.VMEM((ROWS, CELLS), jnp.int32),
        pltpu.SMEM((LEVELS,), jnp.float32),
        pltpu.SMEM((LEVELS,), jnp.float32),
        pltpu.VMEM((4, LEVELS, ROWS, CELLS), jnp.float32),
        pltpu.VMEM((2, 40, CELLS), jnp.float32),
        pltpu.VMEM((2, 40, CELLS), jnp.float32),
        pltpu.VMEM((4, LEVELS, PAD, CELLS), jnp.float32),
        plane,
        plane,
        planes,
        pltpu.VMEM((2, PAD, CELLS), jnp.float32),
        pltpu.VMEM((2, PAD - 16, CELLS), jnp.float32),
        pltpu.VMEM((SLABS - 1, PAD - 16, CELLS), jnp.float32),
        pltpu.VMEM((2, 16, CELLS), jnp.float32),
        pltpu.VMEM((SLABS - 1, 16, CELLS), jnp.float32),
        padded, padded, padded, padded, padded, padded, padded, padded,
        padded, padded, padded, padded,
        pltpu.VMEM((4, LEVELS, PAD, CELLS), jnp.float32),
        padded, padded, padded,
        pltpu.VMEM((8, LEVELS, PAD, CELLS), jnp.float32),
        dma((5,)),
        pltpu.SemaphoreType.REGULAR((4,)),
        dma, dma, dma,
        dma((2,)), dma((2,)), dma((2,)), dma((2,)),
        dma, dma, dma, dma, dma, dma,
    ]
    return pl.pallas_call(
        kernel,
        out_shape=jax.ShapeDtypeStruct(cotangent.shape, jnp.float32),
        in_specs=[pl.BlockSpec(memory_space=pltpu.HBM)] * 6,
        out_specs=pl.BlockSpec(memory_space=pltpu.VMEM),
        scratch_shapes=scratch,
        compiler_params=pltpu.CompilerParams(
            collective_id=0, has_side_effects=True, vmem_limit_bytes=32 << 20
        ),
    )(
        *[
            pltpu.with_memory_space_constraint(x, pltpu.HBM)
            for x in (
                store.reshape(TILES * SLOTS, 4, CELLS), placement, wet, kappa, thickness, cotangent,
            )
        ]
    )


def solution(mesh):
    placed = (
        P("lev", "tile", None, None, None),
        P("lev", "tile"),
        P("tile", None),
        P("lev"),
        P("lev"),
        P(None, "lev", "tile", None),
    )
    return jax.shard_map(
        per_device,
        mesh=mesh,
        in_specs=placed,
        out_specs=P(None, "lev", "tile", None),
        check_vma=False,
    )
```

```python
import functools

import jax
import jax.numpy as jnp
from jax import lax
from jax.experimental import pallas as pl
from jax.experimental.pallas import tpu as pltpu
from jax.sharding import PartitionSpec as P

MESH = pl.DeviceIdType.MESH
LEVELS = 4
ROWS = 64
CELLS = 128
PAD = 72
EDGE = 4
SLOTS = 8
TILES = 64
RING = 16
SIDE = 4
SLABS = 8
HALO = 3
EARLY = (0, 1)
ORDER = (0, 1, 2, 3, 4, 5, 6, 15, 7, 14, 13, 8, 12, 9, 10, 11)
SPLIT = 5
NEAR = 4
UNROLL = True
RIM = 2


def before(x):
    return pltpu.roll(x, 1, 0)


def after(x):
    return pltpu.roll(x, x.shape[0] - 1, 0)


def slope_x(x):
    return 0.5 * (after(x) - before(x))


def slope_y(x):
    return 0.5 * (pltpu.roll(x, CELLS - 1, 1) - pltpu.roll(x, 1, 1))


def stencil(x):
    down, up = after(x), before(x)
    right, left = pltpu.roll(x, CELLS - 1, 1), pltpu.roll(x, 1, 1)
    return 0.5 * (down - up), 0.5 * (right - left), (down + up) + (right + left) - 4.0 * x


def laplace(x):
    return stencil(x)[2]


def kernel(
    store, placement, wet, kappa, thickness, cotangent, out,
    slots, state, halo_out, halo_in, place, wet_in, scale, thick, cot, rim_out, rim_in,
    lam, mask, total, totals, both, mid, mids, edge, edges,
    drive_p, mul_t, mul_s, base_t, base_s, base_u, base_v, bend,
    heat, layer, push_u, push_v, grad, later_t, later_s, adj_q, moved,
    load_sem, ready_sem, slot_send, slot_recv, own_sem, halo_send, halo_recv,
    rim_send, rim_recv, total_send, total_recv, mid_send, mid_recv, edge_send, edge_recv,
):
    me = lax.axis_index("tile")
    lev = lax.axis_index("lev")
    z, y = me // SIDE, lax.rem(me, SIDE)

    def tile_at(dz, dy):
        return lax.rem(z + (dz + RING), RING) * SIDE + lax.rem(y + dy, SIDE)

    def signal(sem, **where):
        pl.semaphore_signal(sem, inc=1, device_id=where, device_id_type=MESH)

    greet = pltpu.get_barrier_semaphore()
    for dz in (1, -1, 2, -2):
        signal(greet, tile=tile_at(dz, 0))
    for dy in (1, 2, 3):
        signal(greet, tile=tile_at(0, dy))
    def nearest_slabs(sem):
        signal(sem, lev=lev + 1 - 2 * lax.rem(lev, 2))
        for k in (2, 4, 6):
            signal(sem, lev=lax.rem(lev + k, SLABS))

    nearest_slabs(greet)

    loads = [
        pltpu.make_async_copy(cotangent, cot, load_sem.at[0]),
        pltpu.make_async_copy(wet, wet_in, load_sem.at[1]),
        pltpu.make_async_copy(placement, place, load_sem.at[2]),
        pltpu.make_async_copy(kappa, scale, load_sem.at[3]),
        pltpu.make_async_copy(thickness, thick, load_sem.at[4]),
    ]
    for load in loads:
        load.start()

    def is_early(plane):
        return functools.reduce(lambda found, e: found | (plane == e), EARLY, plane < 0)

    own = pltpu.make_async_copy(
        store.at[pl.ds(me * SLOTS, SLOTS)], slots.at[pl.ds(me * SLOTS, SLOTS)], own_sem
    )
    own.start()

    def send_slots(to):
        pltpu.make_async_remote_copy(
            src_ref=store.at[pl.ds(to * SLOTS, SLOTS)],
            dst_ref=slots.at[pl.ds(me * SLOTS, SLOTS)],
            send_sem=slot_send,
            recv_sem=slot_recv,
            device_id={"tile": to},
            device_id_type=MESH,
        ).start()

    def send_near(reach):
        for dz in (reach, -reach):
            to_z = lax.rem(z + (dz + RING), RING)

            @pl.when(is_early(to_z) if reach > 2 else z >= 0)
            def _():
                @pl.loop(0 if reach > 2 else 1, SIDE)
                def _(dy):
                    send_slots(tile_at(dz, dy))

    def send_planes(planes):
        for to_z in planes:
            gap = lax.rem(z + (RING - to_z), RING)
            gap = jnp.minimum(gap, RING - gap)

            @pl.when(gap > (NEAR if to_z in EARLY else 2))
            def _():
                @pl.loop(0, SIDE)
                def _(dy):
                    if to_z == RING - 1:

                        @pl.when(dy > 0)
                        def _():
                            send_slots(to_z * SIDE + dy - 1)
                    else:
                        send_slots(to_z * SIDE + lax.rem(y + dy, SIDE))

    pl.semaphore_wait(greet, 7 + 4)
    for dy in (1, 2, 3):
        signal(ready_sem.at[0], tile=tile_at(0, dy))
    for dz in (1, -1, 2, -2):
        send_slots(tile_at(dz, 0))
    for dy in (1, 2, 3):
        send_slots(tile_at(0, dy))
    nearest_slabs(ready_sem.at[3])
    pl.semaphore_wait(ready_sem.at[0], 3)
    for dz in (2, -2):
        signal(ready_sem.at[1], tile=tile_at(dz, 0))
    send_near(1)
    send_near(2)

    pl.semaphore_wait(ready_sem.at[1], 2)
    for dz in (4, -4):
        signal(ready_sem.at[2], tile=tile_at(dz, 0))
    for load in loads:
        load.wait()
    mask[EDGE : EDGE + ROWS] = 0.2 * wet_in[...].astype(jnp.float32)
    rim_out[0, 32:34] = 0.2 * wet_in[0:RIM].astype(jnp.float32)
    rim_out[1, 32:34] = 0.2 * wet_in[ROWS - RIM : ROWS].astype(jnp.float32)
    for f in range(4):
        for l in range(LEVELS):
            i = f * LEVELS + l
            lam[f, l, EDGE : EDGE + ROWS] = cot[f, l]
            rim_out[0, i * RIM : (i + 1) * RIM] = cot[f, l, 0:RIM]
            rim_out[1, i * RIM : (i + 1) * RIM] = cot[f, l, ROWS - RIM : ROWS]

    left, right = lax.rem(me + TILES - 1, TILES), lax.rem(me + 1, TILES)

    def to_neighbours(outgoing, incoming, send, recv):
        return [
            pltpu.make_async_remote_copy(
                src_ref=outgoing.at[side],
                dst_ref=incoming.at[side],
                send_sem=send.at[side],
                recv_sem=recv.at[side],
                device_id={"tile": to},
                device_id_type=MESH,
            )
            for side, to in ((0, left), (1, right))
        ]

    rims = to_neighbours(rim_out, rim_in, rim_send, rim_recv)
    for copy in rims:
        copy.start()

    send_near(3)
    send_near(4)
    pl.semaphore_wait(ready_sem.at[2], 2)
    @pl.when((z < RING - 1 - 2) & (z > 1))
    def _():
        send_slots(TILES - 1)

    send_planes(ORDER[:SPLIT])

    for copy in rims:
        copy.wait_recv()
    for side, at in ((0, EDGE + ROWS), (1, EDGE - RIM)):
        mask[at : at + RIM] = rim_in[side, 32:34]
        for f in range(4):
            for l in range(LEVELS):
                i = f * LEVELS + l
                lam[f, l, at : at + RIM] = rim_in[side, i * RIM : (i + 1) * RIM]

    total[...] = jnp.zeros_like(total)

    @pl.loop(0, LEVELS)
    def _(l):
        m = mask[...]
        p = slope_x(m * lam[2, l]) + slope_y(m * lam[3, l])
        drive_p[l] = p
        total[...] += p

    def to_slabs(source, incoming, send, recv):
        for k in (4, 3, 5, 2, 6, 1, 7):
            to = lax.rem(lev + k, SLABS)
            pltpu.make_async_remote_copy(
                src_ref=source((lev + k) // SLABS),
                dst_ref=incoming.at[k - 1],
                send_sem=send,
                recv_sem=recv,
                device_id={"lev": to},
                device_id_type=MESH,
            ).start()

    def whole(ref, sem):
        pltpu.make_async_copy(ref, ref, sem).wait()

    pl.semaphore_wait(ready_sem.at[3], 4)
    to_slabs(lambda turn: total, totals, total_send, total_recv)

    send_planes(ORDER[SPLIT:])

    whole(totals, total_recv)
    whole(totals, total_send)
    total_above = jnp.zeros((PAD, CELLS), jnp.float32)
    for k in range(1, SLABS):
        total_above += jnp.where(k > lev, totals[k - 1], 0.0)

    def second_step(j, running):
        l = LEVELS - 1 - j
        m = mask[...]
        p = drive_p[l]
        running = running + p
        density = 0.2 * (running - 0.5 * p) * thick[l]
        lt, ls, lu, lv = lam[0, l], lam[1, l], lam[2, l], lam[3, l]
        a, b = m * lt, m * ls
        mul_t[l] = a
        mul_s[l] = b
        for i, x in enumerate((a, b)):
            x = 0.5 * x
            moved[i, l] = after(x)
            moved[i + 2, l] = before(x)
            moved[i + 4, l] = pltpu.roll(x, CELLS - 1, 1)
            moved[i + 6, l] = pltpu.roll(x, 1, 1)
        base_t[l] = lt + scale[l] * laplace(a) - 0.25 * density
        base_s[l] = ls + scale[l] * laplace(b) + 0.75 * density
        base_u[l] = lu - 0.5 * (m * lv)
        base_v[l] = lv + 0.5 * (m * lu)
        bend[l] = 0.1 * density
        return running

    lax.fori_loop(0, LEVELS, second_step, total_above)

    own.wait()
    arrived = slots.at[pl.ds(0, (TILES - 1) * SLOTS)]
    whole(arrived, slot_recv)

    field = LEVELS * PAD
    halos = to_neighbours(halo_out, halo_in, halo_send, halo_recv)
    for side, first in ((1, ROWS - HALO), (0, 0)):
        for l in range(LEVELS):
            for r in range(HALO):
                halo_out[side, l * HALO + r] = slots[place[l, first + r]]
        halos[side].start()

    for l in range(LEVELS):

        @pl.loop(0, ROWS // 8)
        def _(g):
            for r in range(8):
                at = l * PAD + EDGE + g * 8 + r
                state[pl.ds(at, 4, stride=field), :] = slots[place[l, g * 8 + r]]

    def start_field(f, l):
        return state[pl.ds(pl.multiple_of(f * field + l * PAD, 8), PAD), :]

    def first_step(l, cut):
        m = cut(mask[...])
        t, s, u, v = (cut(start_field(f, l)) for f in range(4))
        tx, ty, tl = stencil(t)
        sx, sy, sl = stencil(s)
        t1 = t + m * (scale[l] * tl - u * tx - v * ty)
        s1 = s + m * (scale[l] * sl - u * sx - v * sy)
        q = (-0.25 * t + 0.75 * s - 0.05 * t * t) * thick[l]
        a, b = cut(mul_t[l]), cut(mul_s[l])
        mu = cut(base_u[l]) - a * slope_x(t1) - b * slope_x(s1)
        mv = cut(base_v[l]) - a * slope_y(t1) - b * slope_y(s1)
        c, d = m * mu, m * mv
        p = slope_x(c) + slope_y(d)
        return q, t1, tx, ty, sx, sy, mu - 0.5 * d, mv + 0.5 * c, p

    kept = (
        layer, heat, grad.at[0], grad.at[1], grad.at[2], grad.at[3], push_u, push_v, drive_p,
    )

    mid[...] = jnp.zeros_like(mid)

    @pl.loop(0, LEVELS)
    def _(l):
        values = first_step(l, lambda x: x)
        for ref, value in zip(kept, values):
            ref[l] = value
        mid[0] += values[0][8 : PAD - 8]
        mid[1] += values[-1][8 : PAD - 8]

    to_slabs(lambda turn: mid.at[turn], mids, mid_send, mid_recv)

    for copy in halos:
        copy.wait_recv()
    for side, at in ((0, EDGE + ROWS), (1, EDGE - HALO)):
        for l in range(LEVELS):
            for r in range(HALO):
                state[pl.ds(l * PAD + at + r, 4, stride=field), :] = halo_in[side, l * HALO + r]

    found = [
        first_step(l, lambda x: jnp.concatenate([x[:16], x[PAD - 16 :]], 0)) for l in range(LEVELS)
    ]
    for side, sums in ((0, sum(v[0] for v in found)), (1, sum(v[-1] for v in found))):
        edge[side, :8] = sums[:8]
        edge[side, 8:] = sums[24:]

    to_slabs(lambda turn: edge.at[turn], edges, edge_send, edge_recv)
    for l in range(LEVELS):
        for ref, value in zip(kept, found[l]):
            ref[l, :8] = value[:8]
            ref[l, PAD - 8 :] = value[24:]

    def inner(l, running):
        m = mask[...]
        q = layer[l]
        running = running + q
        pressure = 0.2 * (running - 0.5 * q)
        u, v = start_field(2, l), start_field(3, l)
        u1 = u + m * (0.5 * v - slope_x(pressure))
        v1 = v - m * (0.5 * u + slope_y(pressure))
        a, b = mul_t[l], mul_s[l]
        later_t[l] = base_t[l] - bend[l] * heat[l] + slope_x(a * u1) + slope_y(a * v1)
        later_s[l] = base_s[l] + slope_x(b * u1) + slope_y(b * v1)
        return running

    lax.fori_loop(0, LEVELS, inner, jnp.zeros((PAD, CELLS), jnp.float32))

    def upward(j, running):
        l = LEVELS - 1 - j
        p = drive_p[l]
        running = running + p
        adj_q[l] = running - 0.5 * p
        return running

    lax.fori_loop(0, LEVELS, upward, jnp.zeros((PAD, CELLS), jnp.float32))

    def gather_totals(came):
        upper = jnp.zeros(came.shape[1:], jnp.float32)
        lower = jnp.zeros(came.shape[1:], jnp.float32)
        for k in range(1, SLABS):
            upper += jnp.where(k <= lev, came[k - 1], 0.0)
            lower += jnp.where(k > lev, came[k - 1], 0.0)
        return upper, lower

    whole(mids, mid_recv)
    for i, value in enumerate(gather_totals(mids)):
        both[i, 8 : PAD - 8] = value
    whole(edges, edge_recv)
    for i, value in enumerate(gather_totals(edges)):
        both[i, :8] = value[:8]
        both[i, PAD - 8 :] = value[8:]
    m, upper = mask[...], both[0]
    gx, gy = 0.2 * m * slope_x(upper), 0.2 * m * slope_y(upper)
    totals[0] = after(gx)
    totals[1] = before(gx)
    totals[2] = pltpu.roll(gy, CELLS - 1, 1)
    totals[3] = pltpu.roll(gy, 1, 1)

    def spread(x, u, v, k):
        near, along, across = k * x, 0.5 * (x * u), 0.5 * (x * v)
        rows = after(near + along) + before(near - along)
        cells = pltpu.roll(near + across, CELLS - 1, 1) + pltpu.roll(near - across, 1, 1)
        return rows + cells - 4.0 * near

    @pl.loop(0, LEVELS, unroll=UNROLL)
    def _(l):
        m = mask[...]

        def carried(i):
            down, up = moved[i, l] * totals[0], moved[i + 2, l] * totals[1]
            right, left = moved[i + 4, l] * totals[2], moved[i + 6, l] * totals[3]
            return (down - up) + (right - left)

        mt = later_t[l] - carried(0)
        ms = later_s[l] - carried(1)
        a, b = m * mt, m * ms
        t, u, v = start_field(0, l), start_field(2, l), start_field(3, l)
        density = 0.2 * (adj_q[l] + both[1]) * thick[l]
        here = slice(EDGE, EDGE + ROWS)
        out_t = mt + spread(a, u, v, scale[l]) - density * (0.25 + 0.1 * t)
        out_s = ms + spread(b, u, v, scale[l]) + 0.75 * density
        out_u = push_u[l] - a * grad[0, l] - b * grad[2, l]
        out_v = push_v[l] - a * grad[1, l] - b * grad[3, l]
        out[0, l] = out_t[here]
        out[1, l] = out_s[here]
        out[2, l] = out_u[here]
        out[3, l] = out_v[here]

    for copy in rims + halos:
        copy.wait_send()
    whole(arrived, slot_send)
    whole(mids, mid_send)
    whole(edges, edge_send)


def per_device(store, placement, wet, kappa, thickness, cotangent):
    padded = pltpu.VMEM((LEVELS, PAD, CELLS), jnp.float32)
    plane = pltpu.VMEM((PAD, CELLS), jnp.float32)
    planes = pltpu.VMEM((SLABS - 1, PAD, CELLS), jnp.float32)
    dma = pltpu.SemaphoreType.DMA
    scratch = [
        pltpu.VMEM((TILES * SLOTS, 4, CELLS), jnp.float32),
        pltpu.VMEM((4 * LEVELS * PAD, CELLS), jnp.float32),
        pltpu.VMEM((2, LEVELS * HALO, 4, CELLS), jnp.float32),
        pltpu.VMEM((2, LEVELS * HALO, 4, CELLS), jnp.float32),
        pltpu.SMEM((LEVELS, ROWS), jnp.int32),
        pltpu.VMEM((ROWS, CELLS), jnp.int32),
        pltpu.SMEM((LEVELS,), jnp.float32),
        pltpu.SMEM((LEVELS,), jnp.float32),
        pltpu.VMEM((4, LEVELS, ROWS, CELLS), jnp.float32),
        pltpu.VMEM((2, 40, CELLS), jnp.float32),
        pltpu.VMEM((2, 40, CELLS), jnp.float32),
        pltpu.VMEM((4, LEVELS, PAD, CELLS), jnp.float32),
        plane,
        plane,
        planes,
        pltpu.VMEM((2, PAD, CELLS), jnp.float32),
        pltpu.VMEM((2, PAD - 16, CELLS), jnp.float32),
        pltpu.VMEM((SLABS - 1, PAD - 16, CELLS), jnp.float32),
        pltpu.VMEM((2, 16, CELLS), jnp.float32),
        pltpu.VMEM((SLABS - 1, 16, CELLS), jnp.float32),
        padded, padded, padded, padded, padded, padded, padded, padded,
        padded, padded, padded, padded,
        pltpu.VMEM((4, LEVELS, PAD, CELLS), jnp.float32),
        padded, padded, padded,
        pltpu.VMEM((8, LEVELS, PAD, CELLS), jnp.float32),
        dma((5,)),
        pltpu.SemaphoreType.REGULAR((4,)),
        dma, dma, dma,
        dma((2,)), dma((2,)), dma((2,)), dma((2,)),
        dma, dma, dma, dma, dma, dma,
    ]
    return pl.pallas_call(
        kernel,
        out_shape=jax.ShapeDtypeStruct(cotangent.shape, jnp.float32),
        in_specs=[pl.BlockSpec(memory_space=pltpu.HBM)] * 6,
        out_specs=pl.BlockSpec(memory_space=pltpu.VMEM),
        scratch_shapes=scratch,
        compiler_params=pltpu.CompilerParams(
            collective_id=0, has_side_effects=True, vmem_limit_bytes=32 << 20
        ),
    )(
        *[
            pltpu.with_memory_space_constraint(x, pltpu.HBM)
            for x in (
                store.reshape(TILES * SLOTS, 4, CELLS), placement, wet, kappa, thickness, cotangent,
            )
        ]
    )


def solution(mesh):
    placed = (
        P("lev", "tile", None, None, None),
        P("lev", "tile"),
        P("tile", None),
        P("lev"),
        P("lev"),
        P(None, "lev", "tile", None),
    )
    return jax.shard_map(
        per_device,
        mesh=mesh,
        in_specs=placed,
        out_specs=P(None, "lev", "tile", None),
        check_vma=False,
    )
```
